256 devices in a mesh: grp: 4 (over x), shard: 64 (over z, y, core).
Axes of the slice: x: 4, y: 4, z: 8, core: 2. Of those that a mesh axis runs over, the one named last changes fastest.
Arguments:
- cells: bfloat16 [1024, 64, 768], P('shard'), may hold values from -8 to 8
- w_cell: bfloat16 [768, 768], replicated, may hold values from -0.21875 to 0.21875
- w_mix: bfloat16 [768, 768], replicated, may hold values from -0.21875 to 0.21875
- w_pool: bfloat16 [768, 768], replicated, may hold values from -0.21875 to 0.21875
- pairs: int32 [16384, 2], P(('grp', 'shard')), may hold values from 0 to 1023, as said below
- counts: int32 [256], P(('grp', 'shard')), may hold values from 1 to 64, 12288 in all
Outputs:
- scores: float32 [16384], P(('grp', 'shard'))
The draws below stay inside these ranges and needn't reach their ends.
Inputs may be any that keep to these rules, and one draw needn't show every extreme that they name: Column c lies on shard index c // 16. The first column of each pair of reader r lies on shard index r % 64. Among the 64 pairs of one reader at most 2 have their second column on one shard index, and on some shard index exactly 2. The two columns of a pair differ.
All inputs are finite; a program needn't handle non-finite values. No bound on the sum of `counts` on one device may be relied on, other than what follows from the above.
Results may differ from the reference program's by a relative error of at most 0.0014.
Values may be sent and summed in bfloat16 or wider, within the bound.
A program may use at most 192 MiB of HBM per device.

```python
import math
import jax
import jax.numpy as jnp
import numpy as np
from jax import lax

WIDTH = 768
SAMPLES = 64
COLUMNS_PER_SHARD = 16
PAIR_DEV = 64
COLS = 1024
READERS = 256
PAIRS = 16384
CAP = 2


def draw_cells(key, part):
    base_key = jax.random.fold_in(key, 0)
    value_rows = jnp.clip(jax.random.normal(base_key, (COLS, SAMPLES, WIDTH), jnp.float32), -6.0, 6.0)
    return value_rows.astype(jnp.bfloat16)


def draw_pairs(key, part):
    shards = COLS // COLUMNS_PER_SHARD
    readers = PAIRS // PAIR_DEV

    def one_reader(reader):
        reader_key = jax.random.fold_in(key, reader)
        keys = jax.random.split(reader_key, 6)
        home = reader % shards
        left_local = jax.random.randint(keys[0], (PAIR_DEV,), 0, COLUMNS_PER_SHARD)
        first_owner = jax.random.randint(keys[1], (), 0, shards)
        spread = jax.random.permutation(keys[2], CAP * (shards - 1))[:PAIR_DEV - CAP]
        others = (spread % (shards - 1) + first_owner + 1) % shards
        owners = jnp.concatenate([jnp.full((CAP,), first_owner, jnp.int32), others.astype(jnp.int32)])
        owners = jax.random.permutation(keys[3], owners)
        drawn = jax.random.randint(keys[4], (PAIR_DEV,), 0, COLUMNS_PER_SHARD)
        shifted = (left_local + 1 + jax.random.randint(keys[5], (PAIR_DEV,), 0, COLUMNS_PER_SHARD - 1)) % COLUMNS_PER_SHARD
        right_local = jnp.where(owners == home, shifted, drawn)
        left_ids = home * COLUMNS_PER_SHARD + left_local
        right_ids = owners * COLUMNS_PER_SHARD + right_local
        return jnp.stack([left_ids, right_ids], axis=1)
    return jax.vmap(one_reader)(jnp.arange(readers)).reshape(PAIRS, 2).astype(jnp.int32)


def split_up(number_of, total, limit, skew):
    weights = [(1 << 20) // math.isqrt(rank ** skew) + 1 for rank in range(2, number_of + 1)]
    spare, holding = total - limit - (number_of - 1), [1] * (number_of - 1)
    while spare > 0:
        movable = [i for i in range(number_of - 1) if holding[i] < limit]
        mass, remaining = sum([weights[i] for i in movable]), spare
        for i in movable:
            extra = min(limit - holding[i], max(1, remaining * weights[i] // mass), spare)
            holding[i] = holding[i] + extra
            spare = spare - extra
    return np.array([limit] + holding)


def uneven_parts(rng, count, total, limit, lean):
    if count == 2:
        one = jax.random.randint(rng, (), max(1, total - limit), min(limit, total - 1) + 1)
        return jnp.stack([one, total - one])
    tallies = jnp.asarray(split_up(count, total, limit, lean), jnp.int32)
    pairs = (count - 1) // 2
    giver, sink = tallies[1:1 + 2 * pairs:2], tallies[2:2 + 2 * pairs:2]
    slack = jnp.minimum(giver - 1, limit - sink)
    moved = jax.random.randint(jax.random.fold_in(rng, 1), (pairs,), 0, 1 << 20) % (slack + 1)
    tallies = tallies.at[1:1 + 2 * pairs:2].set(giver - moved).at[2:2 + 2 * pairs:2].set(sink + moved)
    return tallies[jax.random.permutation(jax.random.fold_in(rng, 2), count)]


def noise(stream_key, shape, deviation, limit, kind=jnp.bfloat16):
    entries = jax.random.normal(stream_key, shape, jnp.float32) * deviation
    return jnp.minimum(jnp.maximum(entries, -limit), limit).astype(kind)


def setup_inputs(seed: int = 0) -> dict:
    streams_of = jax.random.split(jax.random.key(seed), 7)
    return {
        "cells": draw_cells(jax.random.fold_in(streams_of[6], 71), 0),
        "w_cell": noise(streams_of[1], (WIDTH, WIDTH), WIDTH ** -0.5, 0.21875),
        "w_mix": noise(streams_of[2], (WIDTH, WIDTH), WIDTH ** -0.5, 0.21875),
        "w_pool": noise(streams_of[3], (WIDTH, WIDTH), WIDTH ** -0.5, 0.21875),
        "pairs": draw_pairs(jax.random.fold_in(streams_of[6], 71), 0),
        "counts": uneven_parts(streams_of[5], READERS, READERS * PAIR_DEV * 3 // 4, PAIR_DEV, 2).astype(jnp.int32),
    }


SOFTMAX_WARMTH = 0.07
EPSILON = 1e-06

def pair_scores(left_block, right_block, w_mix, w_pool):
    left_wide = left_block.astype(jnp.float32)
    right_wide = right_block.astype(jnp.float32)
    score_scale = 1.0 / math.sqrt(left_block.shape[2])
    forward = jnp.einsum('psd,ptd->pst', left_wide, right_wide) * score_scale
    backward = jnp.einsum('ptd,psd->pts', right_wide, left_wide) * score_scale
    attend_left_side = jax.nn.softmax(forward, axis=-1).astype(jnp.bfloat16)
    attend_right = jax.nn.softmax(backward, axis=-1).astype(jnp.bfloat16)
    context_left = jnp.einsum('pst,ptd->psd', attend_left_side.astype(jnp.float32), right_wide)
    context_right = jnp.einsum('pts,psd->ptd', attend_right.astype(jnp.float32), left_wide)
    mixed_left = (left_wide + context_left).astype(jnp.bfloat16)
    mixed_right = (right_wide + context_right).astype(jnp.bfloat16)
    mix_wide = w_mix.astype(jnp.float32)
    pooled_left = lax.optimization_barrier(jnp.mean(jnp.tanh(jnp.einsum('psd,de->pse', mixed_left.astype(jnp.float32), mix_wide)), axis=1)).astype(jnp.bfloat16)
    pooled_right = lax.optimization_barrier(jnp.mean(jnp.tanh(jnp.einsum('psd,de->pse', mixed_right.astype(jnp.float32), mix_wide)), axis=1)).astype(jnp.bfloat16)
    z_left = jnp.dot(pooled_left, w_pool, preferred_element_type=jnp.float32)
    z_right = jnp.dot(pooled_right, w_pool, preferred_element_type=jnp.float32)
    inner_product = lax.optimization_barrier(jnp.mean(z_left * z_right, axis=-1))
    vector_norms = (lax.optimization_barrier(jnp.mean(z_left * z_left, axis=-1)) + EPSILON) * (lax.optimization_barrier(jnp.mean(z_right * z_right, axis=-1)) + EPSILON)
    return inner_product / jnp.sqrt(vector_norms) / SOFTMAX_WARMTH

def reference(cells, w_cell, w_mix, w_pool, pairs, counts):
    projected = jnp.dot(cells.reshape(COLS * SAMPLES, WIDTH), w_cell, preferred_element_type=jnp.float32)
    projected = projected.astype(jnp.bfloat16).reshape(COLS, SAMPLES, WIDTH)
    blocks = pairs.reshape(PAIRS // 8, 8, 2)

    def score_block(block_pairs):
        left_block = jnp.take(projected, block_pairs[:, 0], axis=0)
        right_block = jnp.take(projected, block_pairs[:, 1], axis=0)
        return pair_scores(left_block, right_block, w_mix, w_pool)
    value_rows = lax.map(score_block, blocks).reshape(PAIRS)
    slot_ids = jnp.arange(PAIR_DEV).astype(jnp.int32)
    live = (slot_ids[None, :] < counts[:, None]).reshape(PAIRS)
    return jnp.where(live, value_rows, jnp.zeros_like(value_rows))
```

```python
import functools
import math

import jax
import jax.numpy as jnp
from jax import lax
from jax.experimental import pallas as pl
from jax.experimental.pallas import tpu as pltpu
from jax.sharding import PartitionSpec as P

SOFTMAX_WARMTH = 0.07
EPSILON = 1e-06
MESH = pl.DeviceIdType.MESH
CAPACITY = 512
GROUP = 4


def place():
    x = lax.axis_index("grp")
    shard = lax.axis_index("shard")
    return x, lax.rem(shard // 2, 4), shard // 8, lax.rem(shard, 2)


def gather_kernel(proj, code, sa, sb, plist, stage, send_sem, recv_sem, local_sem):
    x, y, z, core = place()
    shard = lambda z_, y_, c_: z_ * 8 + y_ * 2 + c_
    xr, xl = lax.rem(x + 1, 4), lax.rem(x + 3, 4)
    yr, yl, yo = lax.rem(y + 1, 4), lax.rem(y + 3, 4), lax.rem(y + 2, 4)
    zs = [lax.rem(z + k, 8) for k in range(8)]
    me = shard(z, y, core)
    dev = {
        "x+": (xr, me),
        "x-": (xl, me),
        "y+": (x, shard(z, yr, core)),
        "y-": (x, shard(z, yl, core)),
        "z+": (x, shard(zs[1], y, core)),
        "z-": (x, shard(zs[7], y, core)),
        "c": (x, shard(z, y, 1 - core)),
    }
    barrier = pltpu.get_barrier_semaphore()
    for d in dev.values():
        pl.semaphore_signal(barrier, inc=1, device_id=d, device_id_type=MESH)

    fetch = pltpu.make_async_copy(proj, stage, local_sem.at[0])
    fetch.start()
    fetch.wait()
    pl.semaphore_wait(barrier, len(dev))

    kinds = {}
    sent = []

    def index_of(kind):
        return kinds.setdefault(kind, len(kinds))

    def send(kind, src, dst, to):
        k = index_of(kind)
        copy = pltpu.make_async_remote_copy(
            src_ref=src, dst_ref=dst, send_sem=send_sem.at[k], recv_sem=recv_sem.at[k],
            device_id=dev[to], device_id_type=MESH,
        )
        copy.start()
        sent.append(copy)

    def arrive(kind, slot, to):
        k = index_of(kind)
        pltpu.make_async_remote_copy(
            src_ref=slot, dst_ref=slot, send_sem=send_sem.at[k], recv_sem=recv_sem.at[k],
            device_id=dev[to], device_id_type=MESH,
        ).wait_recv()

    def a_cols(y_, first, size):
        return sa.at[pl.ds(y_ * 16 + first, size)]

    def b_cols(z_, c_, first, size):
        return sb.at[pl.ds(z_ * 8 + c_ * 4 + first, size)]

    keep = [
        pltpu.make_async_copy(stage, a_cols(y, 0, 16), local_sem.at[1]),
        pltpu.make_async_copy(stage.at[pl.ds(4 * x, 4)], b_cols(z, core, 0, 4), local_sem.at[2]),
        pltpu.make_async_copy(code, plist.at[x, y], local_sem.at[3]),
    ]
    send("l+", code, plist.at[x, y], "y+")
    send("l-", code, plist.at[x, y], "y-")
    for p in (0, 1):
        send(f"z+0{p}", stage.at[pl.ds(4 * x + 2 * p, 2)], b_cols(z, core, 2 * p, 2), "z+")
        send(f"z-0{p}", stage.at[pl.ds(4 * x + 2 * (1 - p), 2)], b_cols(z, core, 2 * (1 - p), 2), "z-")
    send("y+S", stage.at[pl.ds(2 * x, 2)], a_cols(y, 2 * x, 2), "y+")
    send("y-S", stage.at[pl.ds(2 * x, 2)], a_cols(y, 2 * x, 2), "y-")
    send("y+D0", stage.at[pl.ds(8, 3)], a_cols(y, 8, 3), "y+")
    send("y-D1", stage.at[pl.ds(11, 5)], a_cols(y, 11, 5), "y-")
    send("c0", stage.at[pl.ds(4 * x, 4)], b_cols(z, core, 0, 4), "c")
    for copy in keep:
        copy.start()

    def z_round(d, p):
        up = b_cols(zs[8 - d], core, 2 * p, 2)
        down = b_cols(zs[d], core, 2 * (1 - p), 2)
        arrive(f"z+{d - 1}{p}", up, "z-")
        if d < 3 or (d == 3 and p == 0):
            send(f"z+{d}{p}", up, up, "z+")
        send(f"c+{d}{p}", up, up, "c")
        arrive(f"z-{d - 1}{p}", down, "z+")
        if d < 3 or (d == 3 and p == 0):
            send(f"z-{d}{p}", down, down, "z-")
        send(f"c-{d}{p}", down, down, "c")

    arrive("l+", plist.at[x, yl], "y-")
    send("l+2", plist.at[x, yl], plist.at[x, yl], "y+")
    arrive("l-", plist.at[x, yr], "y+")

    below, above, far = a_cols(yl, 2 * x, 2), a_cols(yr, 2 * x, 2), a_cols(yo, 2 * x, 2)
    arrive("y+S", below, "y-")
    send("y+S2", below, below, "y+")
    send("x+b", below, below, "x+")
    send("x-b", below, below, "x-")
    arrive("y-S", above, "y+")
    send("x+a", above, above, "x+")
    send("x-a", above, above, "x-")
    send("y+D1", stage.at[pl.ds(11, 5)], a_cols(y, 11, 5), "y+")
    send("y-D0", stage.at[pl.ds(8, 3)], a_cols(y, 8, 3), "y-")
    z_round(1, 0)

    arrive("l+2", plist.at[x, yo], "y-")
    keep[2].wait()
    send("lx+", plist.at[x], plist.at[x], "x+")
    send("lx-", plist.at[x], plist.at[x], "x-")
    z_round(1, 1)

    arrive("y+D0", a_cols(yl, 8, 3), "y-")
    send("y+D02", a_cols(yl, 8, 3), a_cols(yl, 8, 3), "y+")
    got = a_cols(yl, 2 * xl, 2)
    arrive("x+b", got, "x-")
    send("x+b2", got, got, "x+")
    z_round(2, 0)

    arrive("lx+", plist.at[xl], "x-")
    send("lx+2", plist.at[xl], plist.at[xl], "x+")
    got = a_cols(yr, 2 * xr, 2)
    arrive("x-a", got, "x+")
    send("x-a2", got, got, "x-")
    arrive("y-D1", a_cols(yr, 11, 5), "y+")
    send("y-D12", a_cols(yr, 11, 5), a_cols(yr, 11, 5), "y-")
    arrive("y+S2", far, "y-")
    for j in (0, 1):
        one = a_cols(yo, 2 * x + j, 1)
        send(f"x+f{j}", one, one, "x+")
        send(f"x-f{1 - j}", a_cols(yo, 2 * x + 1 - j, 1), a_cols(yo, 2 * x + 1 - j, 1), "x-")
    z_round(2, 1)
    z_round(3, 0)
    got = a_cols(yo, 2 * xl, 1)
    arrive("x+f0", got, "x-")
    send("x+f02", got, got, "x+")
    got = a_cols(yo, 2 * xr + 1, 1)
    arrive("x-f1", got, "x+")
    send("x-f12", got, got, "x-")
    z_round(3, 1)
    z_round(4, 0)

    xo = lax.rem(x + 2, 4)
    arrive("y-D0", a_cols(yr, 8, 3), "y+")
    arrive("y+D1", a_cols(yl, 11, 5), "y-")
    arrive("y+D02", a_cols(yo, 8, 3), "y-")
    arrive("y-D12", a_cols(yo, 11, 5), "y+")
    arrive("x-b", a_cols(yl, 2 * xr, 2), "x+")
    arrive("x+a", a_cols(yr, 2 * xl, 2), "x-")
    arrive("x+b2", a_cols(yl, 2 * xo, 2), "x-")
    arrive("x-a2", a_cols(yr, 2 * xo, 2), "x+")
    arrive("x+f1", a_cols(yo, 2 * xl + 1, 1), "x-")
    arrive("x-f0", a_cols(yo, 2 * xr, 1), "x+")
    arrive("x+f02", a_cols(yo, 2 * xo, 1), "x-")
    arrive("x-f12", a_cols(yo, 2 * xo + 1, 1), "x+")
    arrive("lx-", plist.at[xr], "x+")
    arrive("lx+2", plist.at[xo], "x-")
    other = 1 - core
    arrive("c0", b_cols(z, other, 0, 4), "c")
    for d, p in ((1, 0), (1, 1), (2, 0), (2, 1), (3, 0), (3, 1), (4, 0)):
        arrive(f"c+{d}{p}", b_cols(zs[8 - d], other, 2 * p, 2), "c")
        arrive(f"c-{d}{p}", b_cols(zs[d], other, 2 * (1 - p), 2), "c")
    keep[0].wait()
    keep[1].wait()
    for copy in sent:
        copy.wait_send()
    assert len(kinds) <= COPIES and len(kinds) == len(sent)


COPIES = 80


def gather_blocks(projected, code):
    any_space = pl.BlockSpec(memory_space=pl.ANY)
    columns, samples, features = projected.shape
    return pl.pallas_call(
        gather_kernel,
        out_shape=(
            jax.ShapeDtypeStruct((64, samples, features), jnp.bfloat16),
            jax.ShapeDtypeStruct((64, samples, features), jnp.bfloat16),
            jax.ShapeDtypeStruct((4, 4, 1, 128), jnp.int32),
        ),
        in_specs=[any_space, any_space],
        out_specs=(any_space, any_space, any_space),
        scratch_shapes=[
            pltpu.VMEM((columns, samples, features), jnp.bfloat16),
            pltpu.SemaphoreType.DMA((COPIES,)),
            pltpu.SemaphoreType.DMA((COPIES,)),
            pltpu.SemaphoreType.DMA((4,)),
        ],
        compiler_params=pltpu.CompilerParams(collective_id=0, has_side_effects=True),
        name="gather_blocks",
    )(projected, code)


def score_kernel(
    lst, target, w_mix, w_pool, sa, sb, out, a_buf, b_buf, mixed, pooled, acc, sem
):
    features = w_mix.shape[0]
    samples = a_buf.shape[2]
    scale = 1.0 / math.sqrt(features)
    count = lst[CAPACITY]
    steps = (count + GROUP - 1) // GROUP

    def copies(step, slot):
        found = []
        for j in range(GROUP):
            entry = lst[step * GROUP + j]
            found.append(
                pltpu.make_async_copy(sa.at[entry & 63], a_buf.at[slot, j], sem.at[slot, 0, j])
            )
            found.append(
                pltpu.make_async_copy(sb.at[entry >> 6], b_buf.at[slot, j], sem.at[slot, 1, j])
            )
        return found

    acc[...] = jnp.zeros_like(acc)

    @pl.when(steps > 0)
    def _():
        for copy in copies(0, 0):
            copy.start()

    two = 2 * samples
    same = (
        lax.broadcasted_iota(jnp.int32, (two, two), 0) // samples
        == lax.broadcasted_iota(jnp.int32, (two, two), 1) // samples
    )

    def mix(query, other):
        raw = lax.dot_general(
            query, other, (((1,), (1,)), ((), ())), preferred_element_type=jnp.float32
        )
        raw = jnp.where(same, raw * scale, -1e30)
        raw = raw - jnp.max(raw, axis=-1, keepdims=True)
        weight = jnp.exp(raw)
        attend = (weight / jnp.sum(weight, axis=-1, keepdims=True)).astype(jnp.bfloat16)
        context = jnp.dot(attend, other, preferred_element_type=jnp.float32)
        return (query.astype(jnp.float32) + context).astype(jnp.bfloat16)

    def step_body(step, carry):
        slot = lax.rem(step, 2)

        @pl.when(step + 1 < steps)
        def _():
            for copy in copies(step + 1, 1 - slot):
                copy.start()

        for copy in copies(step, slot):
            copy.wait()
        for h in range(GROUP // 2):
            a = a_buf[slot, pl.ds(2 * h, 2)].reshape(two, features)
            b = b_buf[slot, pl.ds(2 * h, 2)].reshape(two, features)
            mixed[pl.ds(h * two, two)] = mix(a, b)
            mixed[pl.ds(GROUP * samples + h * two, two)] = mix(b, a)
        row = pl.multiple_of(step * 8, 8)
        for first in range(0, features, 256):
            hidden = jnp.tanh(
                jnp.dot(
                    mixed[...], w_mix[:, pl.ds(first, 256)], preferred_element_type=jnp.float32
                )
            )
            mean = jnp.sum(hidden.reshape(2 * GROUP, samples, 256), axis=1) * (1.0 / samples)
            pooled[pl.ds(row, 8), pl.ds(first, 256)] = mean
        return carry

    lax.fori_loop(0, steps, step_body, 0)

    def finish(chunk, carry):
        row = pl.multiple_of(chunk * 256, 256)
        vectors = pooled[pl.ds(row, 256)].astype(jnp.bfloat16)
        right = jnp.dot(vectors, w_pool[...], preferred_element_type=jnp.float32)
        left = pltpu.roll(right, 4, 0)
        inner = jnp.mean(left * right, axis=-1, keepdims=True)
        norms = (jnp.mean(left * left, axis=-1, keepdims=True) + EPSILON) * (
            jnp.mean(right * right, axis=-1, keepdims=True) + EPSILON
        )
        score = inner / jnp.sqrt(norms) / SOFTMAX_WARMTH
        hit = target[...] == row + lax.broadcasted_iota(jnp.int32, (256, 1024), 0)
        acc[...] += jnp.sum(jnp.where(hit, score, 0.0), axis=0, keepdims=True)
        return carry

    lax.fori_loop(0, (steps + 31) // 32, finish, 0)
    for k in range(8):
        out[k] = acc[:, pl.ds(128 * k, 128)]


def score_pairs(lst, target, w_mix, w_pool, sa, sb):
    samples, features = sa.shape[1:]
    vmem = pl.BlockSpec(memory_space=pltpu.VMEM)
    any_space = pl.BlockSpec(memory_space=pl.ANY)
    return pl.pallas_call(
        score_kernel,
        out_shape=jax.ShapeDtypeStruct((8, 1, 128), jnp.float32),
        in_specs=[
            pl.BlockSpec(memory_space=pltpu.SMEM), vmem, vmem, vmem, any_space, any_space,
        ],
        out_specs=vmem,
        scratch_shapes=[
            pltpu.VMEM((2, GROUP, samples, features), jnp.bfloat16),
            pltpu.VMEM((2, GROUP, samples, features), jnp.bfloat16),
            pltpu.VMEM((2 * GROUP * samples, features), jnp.bfloat16),
            pltpu.VMEM((2 * CAPACITY, features), jnp.float32),
            pltpu.VMEM((1, 1024), jnp.float32),
            pltpu.SemaphoreType.DMA((2, 2, GROUP)),
        ],
        name="score_pairs",
    )(lst, target, w_mix, w_pool, sa, sb)


def return_kernel(part, out, landed, send_sem, recv_sem):
    x, y, z, core = place()
    me = z * 8 + y * 2 + core

    def partner(k):
        return lax.rem(x + k // 4, 4), lax.rem(y + k % 4, 4)

    barrier = pltpu.get_barrier_semaphore()
    for k in range(1, 16):
        tx, ty = partner(k)
        pl.semaphore_signal(
            barrier, inc=1, device_id=(tx, z * 8 + ty * 2 + core), device_id_type=MESH
        )
    pl.semaphore_wait(barrier, 15)
    sent = []
    for k in range(1, 16):
        tx, ty = partner(k)
        copy = pltpu.make_async_remote_copy(
            src_ref=part.at[tx * 2 + ty // 2], dst_ref=landed.at[k],
            send_sem=send_sem.at[k], recv_sem=recv_sem.at[k],
            device_id=(tx, z * 8 + ty * 2 + core), device_id_type=MESH,
        )
        copy.start()
        sent.append(copy)
    total = part[x * 2 + y // 2]
    for k, copy in enumerate(sent, start=1):
        copy.wait_recv()
        total = total + landed[k]
    out[...] = total
    for copy in sent:
        copy.wait_send()


def return_scores(part):
    vmem = pl.BlockSpec(memory_space=pltpu.VMEM)
    return pl.pallas_call(
        return_kernel,
        out_shape=jax.ShapeDtypeStruct((1, 128), jnp.float32),
        in_specs=[vmem],
        out_specs=vmem,
        scratch_shapes=[
            pltpu.VMEM((16, 1, 128), jnp.float32),
            pltpu.SemaphoreType.DMA((16,)),
            pltpu.SemaphoreType.DMA((16,)),
        ],
        compiler_params=pltpu.CompilerParams(collective_id=1, has_side_effects=True),
        name="return_scores",
    )(part)


def my_pairs(plist):
    x, y, _, _ = place()
    codes = plist[:, :, 0, :64].reshape(1024)
    b = codes >> 6
    mine = (codes >= 0) & (((b >> 5) & 3) == y) & (((b >> 2) & 3) == x)
    entry = (codes & 63) + 64 * ((b >> 7) * 8 + ((b >> 4) & 1) * 4 + (b & 3))
    slot = jnp.arange(1024, dtype=jnp.int32)
    before = jnp.sum(jnp.where((slot[None, :] < slot[:, None]) & mine[None, :], 1, 0), axis=1)
    position = jnp.where(mine, before, -1)
    order = jnp.arange(CAPACITY, dtype=jnp.int32)
    entries = jnp.sum(jnp.where(position[None, :] == order[:, None], entry[None, :], 0), axis=1)
    count = jnp.sum(jnp.where(mine, 1, 0))
    target = jnp.where(mine, 8 * (before // GROUP) + 4 + before % GROUP, -1)
    lst = jnp.concatenate([entries, count[None], jnp.zeros((7,), jnp.int32)])
    return lst.astype(jnp.int32), target.reshape(1, 1024).astype(jnp.int32)


def local(cells, w_cell, w_mix, w_pool, pairs, counts):
    columns, samples, features = cells.shape
    pair_dev = pairs.shape[0]
    projected = jnp.dot(
        cells.reshape(columns * samples, features), w_cell, preferred_element_type=jnp.float32
    )
    projected = projected.astype(jnp.bfloat16).reshape(columns, samples, features)
    x, y, _, _ = place()
    slot = jnp.arange(pair_dev, dtype=jnp.int32)
    code = y * 16 + pairs[:, 0] % columns + 64 * pairs[:, 1]
    code = jnp.where(slot < counts[0], code, -1)
    code = jnp.concatenate([code, jnp.full((128 - pair_dev,), -1, jnp.int32)]).reshape(1, 128)
    sa, sb, plist = gather_blocks(projected, code)
    lst, target = my_pairs(plist)
    part = score_pairs(lst, target, w_mix, w_pool, sa, sb)
    whole = return_scores(part).reshape(128)
    return jnp.where(lax.rem(y, 2) == 0, whole[:64], whole[64:])


def solution(mesh):
    placed = (P("shard", None, None), P(), P(), P(), P(("grp", "shard"), None), P(("grp", "shard")))
    return jax.shard_map(
        local, mesh=mesh, in_specs=placed, out_specs=P(("grp", "shard")), check_vma=False
    )
```

```python
import functools
import math

import jax
import jax.numpy as jnp
from jax import lax
from jax.experimental import pallas as pl
from jax.experimental.pallas import tpu as pltpu
from jax.sharding import PartitionSpec as P

SOFTMAX_WARMTH = 0.07
EPSILON = 1e-06
MESH = pl.DeviceIdType.MESH
CAPACITY = 512
GROUP = 4


def place():
    x = lax.axis_index("grp")
    shard = lax.axis_index("shard")
    return x, lax.rem(shard // 2, 4), shard // 8, lax.rem(shard, 2)


def gather_kernel(
    cells, w_cell, w_mix, code, sa, sb, sa_mix, sb_mix, plist, stage, cell_w, mix_w,
    send_sem, recv_sem, local_sem
):
    columns, samples, features = stage.shape
    x, y, z, core = place()
    shard = lambda z_, y_, c_: z_ * 8 + y_ * 2 + c_
    xr, xl = lax.rem(x + 1, 4), lax.rem(x + 3, 4)
    yr, yl, yo = lax.rem(y + 1, 4), lax.rem(y + 3, 4), lax.rem(y + 2, 4)
    zs = [lax.rem(z + k, 8) for k in range(8)]
    me = shard(z, y, core)
    dev = {
        "x+": (xr, me),
        "x-": (xl, me),
        "y+": (x, shard(z, yr, core)),
        "y-": (x, shard(z, yl, core)),
        "z+": (x, shard(zs[1], y, core)),
        "z-": (x, shard(zs[7], y, core)),
        "c": (x, shard(z, y, 1 - core)),
    }
    barrier = pltpu.get_barrier_semaphore()
    for d in dev.values():
        pl.semaphore_signal(barrier, inc=1, device_id=d, device_id_type=MESH)

    loads = [
        pltpu.make_async_copy(cells, stage, local_sem.at[0]),
        pltpu.make_async_copy(w_cell, cell_w, local_sem.at[1]),
        pltpu.make_async_copy(w_mix, mix_w, local_sem.at[2]),
        pltpu.make_async_copy(code, plist.at[x, y], local_sem.at[3]),
    ]
    for copy in loads:
        copy.start()
    def project(quarter):
        rows = stage[pl.ds(quarter * 4, 4)].reshape(4 * samples, features)
        for first in range(0, features, 256):
            block = jnp.dot(
                rows, cell_w[:, pl.ds(first, 256)], preferred_element_type=jnp.float32
            ).astype(jnp.bfloat16)
            sa[pl.ds(y * 16 + quarter * 4, 4), :, pl.ds(first, 256)] = block.reshape(4, samples, 256)

    loads[0].wait()
    loads[1].wait()
    project(x)
    sb[pl.ds(z * 8 + core * 4, 4)] = sa[pl.ds(y * 16 + 4 * x, 4)]
    pl.semaphore_wait(barrier, len(dev))

    def times_mix(source, result, runs):
        rows = jnp.concatenate([source[pl.ds(*run)] for run in runs], axis=0)
        rows = rows.reshape(-1, features)
        for first in range(0, features, 256):
            block = jnp.dot(
                rows, mix_w[:, pl.ds(first, 256)], preferred_element_type=jnp.float32
            ).astype(jnp.bfloat16).reshape(-1, samples, 256)
            at = 0
            for start, size in runs:
                result[pl.ds(start, size), :, pl.ds(first, 256)] = block[at : at + size]
                at += size

    def mix_a(first_y, step_y, count, half):
        def body(k, carry):
            base = lax.rem(first_y + step_y * k, 4) * 16 + 2 * half
            times_mix(sa, sa_mix, [(base + 4 * q, 2) for q in range(4)])
            return carry
        lax.fori_loop(0, count, body, 0)

    def mix_b(d):
        def body(k, carry):
            times_mix(sb, sb_mix, [(lax.rem(z + 8 - d + 2 * d * k, 8) * 8, 8)])
            return carry
        lax.fori_loop(0, 1 if d in (0, 4) else 2, body, 0)

    kinds = {}
    sent = []

    def index_of(kind):
        return kinds.setdefault(kind, len(kinds))

    def send(kind, src, dst, to):
        k = index_of(kind)
        copy = pltpu.make_async_remote_copy(
            src_ref=src, dst_ref=dst, send_sem=send_sem.at[k], recv_sem=recv_sem.at[k],
            device_id=dev[to], device_id_type=MESH,
        )
        copy.start()
        sent.append(copy)

    def arrive(kind, slot, to):
        k = index_of(kind)
        pltpu.make_async_remote_copy(
            src_ref=slot, dst_ref=slot, send_sem=send_sem.at[k], recv_sem=recv_sem.at[k],
            device_id=dev[to], device_id_type=MESH,
        ).wait_recv()

    def a_cols(y_, first, size):
        return sa.at[pl.ds(y_ * 16 + first, size)]

    def b_cols(z_, c_, first, size):
        return sb.at[pl.ds(z_ * 8 + c_ * 4 + first, size)]

    def direct(y_, k):
        return a_cols(y_, 4 * lax.rem(x + k, 4) + 2, 2)

    def last(y_, k):
        return a_cols(y_, 4 * lax.rem(x + k, 4) + 3, 1)

    shared = a_cols(y, 4 * x, 2)
    loads[3].wait()
    send("l+", plist.at[x, y], plist.at[x, y], "y+")
    send("l-", plist.at[x, y], plist.at[x, y], "y-")
    for p in (0, 1):
        send(f"z+0{p}", b_cols(z, core, 2 * p, 2), b_cols(z, core, 2 * p, 2), "z+")
        send(f"z-0{p}", b_cols(z, core, 2 * (1 - p), 2), b_cols(z, core, 2 * (1 - p), 2), "z-")
        if p == 0:
            send("y+S", shared, shared, "y+")
            send("y-S", shared, shared, "y-")
    send("y+D0", direct(y, 0), direct(y, 0), "y+")
    send("y-D0", direct(y, 0), direct(y, 0), "y-")
    send("c0", b_cols(z, core, 0, 4), b_cols(z, core, 0, 4), "c")
    project(lax.rem(x + 1, 4))
    send("y+D1", direct(y, 1), direct(y, 1), "y+")
    send("y-D1", direct(y, 1), direct(y, 1), "y-")
    project(lax.rem(x + 2, 4))
    project(lax.rem(x + 3, 4))
    loads[2].wait()
    other = 1 - core
    arrive_c0 = lambda: arrive("c0", b_cols(z, other, 0, 4), "c")

    def arrive_c(d, p):
        arrive(f"c+{d}{p}", b_cols(zs[8 - d], other, 2 * p, 2), "c")
        arrive(f"c-{d}{p}", b_cols(zs[d], other, 2 * (1 - p), 2), "c")

    def z_round(d, p):
        up = b_cols(zs[8 - d], core, 2 * p, 2)
        down = b_cols(zs[d], core, 2 * (1 - p), 2)
        arrive(f"z+{d - 1}{p}", up, "z-")
        if d < 3 or (d == 3 and p == 0):
            send(f"z+{d}{p}", up, up, "z+")
        send(f"c+{d}{p}", up, up, "c")
        arrive(f"z-{d - 1}{p}", down, "z+")
        if d < 3 or (d == 3 and p == 0):
            send(f"z-{d}{p}", down, down, "z-")
        send(f"c-{d}{p}", down, down, "c")

    mix_a(y, 0, 1, 0)
    mix_a(y, 0, 1, 1)
    arrive_c0()
    mix_b(0)

    below, above = a_cols(yl, 4 * x, 2), a_cols(yr, 4 * x, 2)
    arrive("l+", plist.at[x, yl], "y-")
    send("l+2", plist.at[x, yl], plist.at[x, yl], "y+")
    arrive("l-", plist.at[x, yr], "y+")
    arrive("y+S", below, "y-")
    send("y+S2", below, below, "y+")
    send("x+b", below, below, "x+")
    send("x-b", below, below, "x-")
    arrive("y-S", above, "y+")
    send("x+a", above, above, "x+")
    send("x-a", above, above, "x-")
    z_round(1, 0)

    arrive("y+D0", direct(yl, 0), "y-")
    send("y+c", a_cols(yl, 4 * x + 2, 1), a_cols(yl, 4 * x + 2, 1), "y+")
    send("y+D2", direct(y, 2), direct(y, 2), "y+")
    send("y+D3", direct(y, 3), direct(y, 3), "y+")
    arrive("y-D0", direct(yr, 0), "y+")
    send("y-r0", last(yr, 0), last(yr, 0), "y-")
    send("y-D2", direct(y, 2), direct(y, 2), "y-")
    z_round(1, 1)
    arrive("l+2", plist.at[x, yo], "y-")
    send("lx+", plist.at[x], plist.at[x], "x+")
    send("lx-", plist.at[x], plist.at[x], "x-")

    got = a_cols(yl, 4 * xl, 2)
    arrive("x+b", got, "x-")
    send("x+b2", got, got, "x+")
    arrive_c(1, 0)
    arrive_c(1, 1)
    mix_b(1)
    z_round(2, 0)
    arrive("y-D1", direct(yr, 1), "y+")
    send("y-r1", last(yr, 1), last(yr, 1), "y-")
    send("y-D3", direct(y, 3), direct(y, 3), "y-")
    got = a_cols(yr, 4 * xr, 2)
    arrive("x-a", got, "x+")
    send("x-a2", got, got, "x-")
    arrive("lx+", plist.at[xl], "x-")
    send("lx+2", plist.at[xl], plist.at[xl], "x+")
    z_round(2, 1)

    arrive("y+S2", a_cols(yo, 4 * x, 2), "y-")
    for j in (0, 1):
        one, two = a_cols(yo, 4 * x + j, 1), a_cols(yo, 4 * x + 1 - j, 1)
        send(f"x+f{j}", one, one, "x+")
        send(f"x-f{1 - j}", two, two, "x-")
    arrive_c(2, 0)
    arrive_c(2, 1)
    mix_b(2)
    arrive("y+c", a_cols(yo, 4 * x + 2, 1), "y-")
    for to in ("x+", "x-"):
        send(to + "c", a_cols(yo, 4 * x + 2, 1), a_cols(yo, 4 * x + 2, 1), to)
    arrive("y-D2", direct(yr, 2), "y+")
    send("y-r2", last(yr, 2), last(yr, 2), "y-")
    z_round(3, 0)
    xo = lax.rem(x + 2, 4)
    arrive("x-b", a_cols(yl, 4 * xr, 2), "x+")
    arrive("x+a", a_cols(yr, 4 * xl, 2), "x-")
    arrive("x+b2", a_cols(yl, 4 * xo, 2), "x-")
    arrive("x-a2", a_cols(yr, 4 * xo, 2), "x+")
    got = a_cols(yo, 4 * xl, 1)
    arrive("x+f0", got, "x-")
    send("x+f02", got, got, "x+")
    got = a_cols(yo, 4 * xr + 1, 1)
    arrive("x-f1", got, "x+")
    send("x-f12", got, got, "x-")
    mix_a(yl, 2, 2, 0)
    z_round(3, 1)
    arrive("y-D3", direct(yr, 3), "y+")
    send("y-r3", last(yr, 3), last(yr, 3), "y-")
    got = a_cols(yo, 4 * xl + 2, 1)
    arrive("x+c", got, "x-")
    send("x+c2", got, got, "x+")
    mix_a(yr, 0, 1, 1)
    arrive_c(3, 0)
    arrive_c(3, 1)
    mix_b(3)
    for k in (1, 2, 3):
        arrive(f"y+D{k}", direct(yl, k), "y-")
    mix_a(yl, 0, 1, 1)

    z_round(4, 0)
    arrive("x+f1", a_cols(yo, 4 * xl + 1, 1), "x-")
    arrive("x-f0", a_cols(yo, 4 * xr, 1), "x+")
    arrive("x+f02", a_cols(yo, 4 * xo, 1), "x-")
    arrive("x-f12", a_cols(yo, 4 * xo + 1, 1), "x+")
    mix_a(yo, 0, 1, 0)
    arrive("x-c", a_cols(yo, 4 * xr + 2, 1), "x+")
    arrive("x+c2", a_cols(yo, 4 * xo + 2, 1), "x-")
    for k in range(4):
        arrive(f"y-r{k}", last(yo, k), "y+")
    mix_a(yo, 0, 1, 1)
    arrive_c(4, 0)
    mix_b(4)
    arrive("lx-", plist.at[xr], "x+")
    arrive("lx+2", plist.at[xo], "x-")
    for copy in sent:
        copy.wait_send()
    assert len(kinds) <= COPIES and len(kinds) == len(sent)


COPIES = 96


def gather_blocks(cells, w_cell, w_mix, code):
    vmem = pl.BlockSpec(memory_space=pltpu.VMEM)
    columns, samples, features = cells.shape
    blocks = pltpu.VMEM((64, samples, features), jnp.bfloat16)
    return pl.pallas_call(
        gather_kernel,
        out_shape=(blocks,) * 4 + (pltpu.VMEM((4, 4, 1, 128), jnp.int32),),
        in_specs=[pl.BlockSpec(memory_space=pltpu.HBM)] * 3 + [vmem],
        out_specs=(vmem,) * 5,
        scratch_shapes=[
            pltpu.VMEM((columns, samples, features), jnp.bfloat16),
            pltpu.VMEM(w_cell.shape, jnp.bfloat16),
            pltpu.VMEM(w_mix.shape, jnp.bfloat16),
            pltpu.SemaphoreType.DMA((COPIES,)),
            pltpu.SemaphoreType.DMA((COPIES,)),
            pltpu.SemaphoreType.DMA((4,)),
        ],
        compiler_params=pltpu.CompilerParams(
            collective_id=0, has_side_effects=True, vmem_limit_bytes=12 << 20
        ),
        name="gather_blocks",
    )(cells, w_cell, w_mix, code)


def score_kernel(
    sa, sb, sa_mix, sb_mix, plist, w_pool, out,
    pool_w, blend, pooled, target, table, lst, sem, list_sem
):
    samples, features = sa.shape[1:]
    scale = 1.0 / math.sqrt(features)
    load = pltpu.make_async_copy(w_pool, pool_w, sem)
    load.start()

    x, y, _, _ = place()
    codes = jnp.concatenate(
        [jnp.maximum(plist[k // 2, k % 2 * 2], plist[k // 2, k % 2 * 2 + 1]) for k in range(8)],
        axis=0,
    )
    b_id = codes >> 6
    mine = (codes >= 0) & (((b_id >> 5) & 3) == y) & (((b_id >> 2) & 3) == x)
    flag = jnp.where(mine, 1.0, 0.0)
    row_id = lax.broadcasted_iota(jnp.int32, (8, 128), 0)
    lane = lambda n: lax.broadcasted_iota(jnp.int32, (128, n), 1)
    upto = jnp.where(lax.broadcasted_iota(jnp.int32, (128, 128), 0) < lane(128), 1.0, 0.0)
    ahead = jnp.dot(
        flag.astype(jnp.bfloat16), upto.astype(jnp.bfloat16), preferred_element_type=jnp.float32
    )
    rows_upto = jnp.broadcast_to(jnp.sum(flag, axis=1, keepdims=True), (8, 128))
    own = rows_upto
    for shift in (1, 2, 4):
        rows_upto = rows_upto + jnp.where(
            row_id >= shift, pltpu.roll(rows_upto, shift, 0), 0.0
        )
    position = jnp.where(mine, (ahead + rows_upto - own).astype(jnp.int32), -1)
    target[...] = jnp.where(
        mine, 8 * (position >> 2) + 4 * ((position >> 1) & 1) + 2 + (position & 1), -1
    )
    spread = position.T
    a_at = (codes & 63).astype(jnp.bfloat16)
    b_at = ((b_id >> 7) * 8 + ((b_id >> 4) & 1) * 4 + (b_id & 3)).astype(jnp.bfloat16)
    found_a = jnp.zeros((8, CAPACITY), jnp.float32)
    found_b = jnp.zeros((8, CAPACITY), jnp.float32)
    for k in range(8):
        hit = jnp.where(spread[:, k : k + 1] == lane(CAPACITY), 1.0, 0.0).astype(jnp.bfloat16)
        keep = row_id == k
        both = jnp.concatenate(
            [jnp.where(keep, a_at, 0), jnp.where(keep, b_at, 0)], axis=0
        ).astype(jnp.bfloat16)
        got = jnp.dot(both, hit, preferred_element_type=jnp.float32)
        found_a = found_a + got[:8]
        found_b = found_b + got[8:]
    sum_rows = lambda v: jnp.sum(v, axis=0, keepdims=True).astype(jnp.int32)
    total = jnp.broadcast_to(rows_upto[7:, :1], (1, CAPACITY)).astype(jnp.int32)
    table[0] = sum_rows(found_a)
    table[1] = sum_rows(found_b)
    table[2] = total
    move = pltpu.make_async_copy(table, lst, list_sem)
    move.start()
    move.wait()
    count = lst[2, 0, 0]
    steps = (count + GROUP - 1) // GROUP

    two = 2 * samples
    same = (
        lax.broadcasted_iota(jnp.int32, (two, two), 0) // samples
        == lax.broadcasted_iota(jnp.int32, (two, two), 1) // samples
    )
    identity = jnp.where(
        lax.broadcasted_iota(jnp.int32, (two, two), 0) == lax.broadcasted_iota(jnp.int32, (two, two), 1),
        1.0, 0.0,
    ).astype(jnp.bfloat16)
    for h in range(GROUP // 2):
        blend[h, pl.ds(0, two), pl.ds(0, two)] = identity
        blend[h, pl.ds(two, two), pl.ds(two, two)] = identity

    def pair_rows(source, which, step, h):
        first = step * GROUP + 2 * h
        return jnp.concatenate(
            [source[lst[which, 0, first]], source[lst[which, 0, first + 1]]], axis=0
        )

    def scores(step, h):
        raw = lax.dot_general(
            pair_rows(sa, 0, step, h), pair_rows(sb, 1, step, h), (((1,), (1,)), ((), ())),
            preferred_element_type=jnp.float32,
        )
        return jnp.where(same, raw * scale, -1e30)

    def attend(raw, axis):
        weight = jnp.exp(raw - jnp.max(raw, axis=axis, keepdims=True))
        return weight * (1.0 / jnp.sum(weight, axis=axis, keepdims=True))

    def keep_weights(raw, h):
        blend[h, pl.ds(0, two), pl.ds(two, two)] = attend(raw, 1).astype(jnp.bfloat16)
        blend[h, pl.ds(two, two), pl.ds(0, two)] = attend(raw, 0).T.astype(jnp.bfloat16)

    def pool(step):
        products = [
            jnp.concatenate(
                [pair_rows(sa_mix, 0, step, h), pair_rows(sb_mix, 1, step, h)], axis=0
            )
            for h in range(GROUP // 2)
        ]
        row = pl.multiple_of(step * 2 * GROUP, 2 * GROUP)
        for first in range(0, features, 256):
            means = []
            for h in range(GROUP // 2):
                hidden = jnp.tanh(
                    jnp.dot(
                        blend[h], products[h][:, first : first + 256],
                        preferred_element_type=jnp.float32,
                    )
                )
                means.append(jnp.sum(hidden.reshape(4, samples, 256), axis=1) * (1.0 / samples))
            pooled[pl.ds(row, 2 * GROUP), pl.ds(first, 256)] = jnp.concatenate(means, axis=0)

    def step_body(step, carry):
        raw = [scores(step, h) for h in range(GROUP // 2)]
        pool(step - 1)
        for h in range(GROUP // 2):
            keep_weights(raw[h], h)
        return carry

    @pl.when(steps > 0)
    def _():
        raw = [scores(0, h) for h in range(GROUP // 2)]
        for h in range(GROUP // 2):
            keep_weights(raw[h], h)
        lax.fori_loop(1, steps, step_body, 0)
        pool(steps - 1)

    load.wait()
    out[...] = jnp.zeros_like(out)

    def finish(chunk, carry):
        row = pl.multiple_of(chunk * 256, 256)
        vectors = pooled[pl.ds(row, 256)].astype(jnp.bfloat16)
        right = jnp.dot(vectors, pool_w[...], preferred_element_type=jnp.float32)
        left = pltpu.roll(right, 2, 0)
        inner = jnp.mean(left * right, axis=-1, keepdims=True)
        norms = (jnp.mean(left * left, axis=-1, keepdims=True) + EPSILON) * (
            jnp.mean(right * right, axis=-1, keepdims=True) + EPSILON
        )
        score = inner / jnp.sqrt(norms) / SOFTMAX_WARMTH
        number = row + lax.broadcasted_iota(jnp.int32, (256, 128), 0)
        for k in range(8):
            hit = target[pl.ds(k, 1)] == number
            out[k] += jnp.sum(jnp.where(hit, score, 0.0), axis=0, keepdims=True)
        return carry

    lax.fori_loop(0, (steps + 31) // 32, finish, 0)


def score_pairs(sa, sb, sa_mix, sb_mix, plist, w_pool):
    samples, features = sa.shape[1:]
    vmem = pl.BlockSpec(memory_space=pltpu.VMEM)
    two = 2 * samples
    return pl.pallas_call(
        score_kernel,
        out_shape=pltpu.VMEM((8, 1, 128), jnp.float32),
        in_specs=[vmem] * 5 + [pl.BlockSpec(memory_space=pltpu.HBM)],
        out_specs=vmem,
        scratch_shapes=[
            pltpu.VMEM(w_pool.shape, jnp.bfloat16),
            pltpu.VMEM((GROUP // 2, 2 * two, 2 * two), jnp.bfloat16),
            pltpu.VMEM((2 * CAPACITY, features), jnp.float32),
            pltpu.VMEM((8, 128), jnp.int32),
            pltpu.VMEM((3, 1, CAPACITY), jnp.int32),
            pltpu.SMEM((3, 1, CAPACITY), jnp.int32),
            pltpu.SemaphoreType.DMA,
            pltpu.SemaphoreType.DMA,
        ],
        compiler_params=pltpu.CompilerParams(vmem_limit_bytes=16 << 20),
        name="score_pairs",
    )(sa, sb, sa_mix, sb_mix, plist, w_pool)


def return_kernel(part, out, landed, send_sem, recv_sem):
    x, y, z, core = place()
    me = z * 8 + y * 2 + core

    def partner(k):
        return lax.rem(x + k // 4, 4), lax.rem(y + k % 4, 4)

    barrier = pltpu.get_barrier_semaphore()
    for k in range(1, 16):
        tx, ty = partner(k)
        pl.semaphore_signal(
            barrier, inc=1, device_id=(tx, z * 8 + ty * 2 + core), device_id_type=MESH
        )
    pl.semaphore_wait(barrier, 15)
    sent = []
    for k in range(1, 16):
        tx, ty = partner(k)
        copy = pltpu.make_async_remote_copy(
            src_ref=part.at[tx * 2 + ty // 2], dst_ref=landed.at[k],
            send_sem=send_sem.at[k], recv_sem=recv_sem.at[k],
            device_id=(tx, z * 8 + ty * 2 + core), device_id_type=MESH,
        )
        copy.start()
        sent.append(copy)
    total = part[x * 2 + y // 2]
    for k, copy in enumerate(sent, start=1):
        copy.wait_recv()
        total = total + landed[k]
    half = jnp.where(lax.rem(y, 2) == 0, total, pltpu.roll(total, 64, 1))
    out[...] = half[:, :64]
    for copy in sent:
        copy.wait_send()


def return_scores(part):
    vmem = pl.BlockSpec(memory_space=pltpu.VMEM)
    return pl.pallas_call(
        return_kernel,
        out_shape=jax.ShapeDtypeStruct((1, 64), jnp.float32),
        in_specs=[vmem],
        out_specs=vmem,
        scratch_shapes=[
            pltpu.VMEM((16, 1, 128), jnp.float32),
            pltpu.SemaphoreType.DMA((16,)),
            pltpu.SemaphoreType.DMA((16,)),
        ],
        compiler_params=pltpu.CompilerParams(
            collective_id=1, has_side_effects=True, vmem_limit_bytes=1 << 20
        ),
        name="return_scores",
    )(part)


def local(cells, w_cell, w_mix, w_pool, pairs, counts):
    columns = cells.shape[0]
    pair_dev = pairs.shape[0]
    _, y, _, _ = place()
    slot = jnp.arange(pair_dev, dtype=jnp.int32)
    code = y * 16 + pairs[:, 0] % columns + 64 * pairs[:, 1]
    code = jnp.where(slot < counts[0], code, -1)
    odd = lax.rem(y, 2)
    code = jnp.concatenate([jnp.where(odd == 0, code, -1), jnp.where(odd == 1, code, -1)])
    cells, w_cell, w_mix, w_pool = [
        pltpu.with_memory_space_constraint(v, pltpu.HBM) for v in (cells, w_cell, w_mix, w_pool)
    ]
    blocks = gather_blocks(cells, w_cell, w_mix, code.reshape(1, 128))
    return return_scores(score_pairs(*blocks, w_pool)).reshape(pair_dev)


def solution(mesh):
    placed = (P("shard", None, None), P(), P(), P(), P(("grp", "shard"), None), P(("grp", "shard")))
    return jax.shard_map(
        local, mesh=mesh, in_specs=placed, out_specs=P(("grp", "shard")), check_vma=False
    )
```

```python
import functools
import math

import jax
import jax.numpy as jnp
from jax import lax
from jax.experimental import pallas as pl
from jax.experimental.pallas import tpu as pltpu
from jax.sharding import PartitionSpec as P

SOFTMAX_WARMTH = 0.07
EPSILON = 1e-06
MESH = pl.DeviceIdType.MESH
CAPACITY = 512
GROUP = 4


def place():
    x = lax.axis_index("grp")
    shard = lax.axis_index("shard")
    return x, lax.rem(shard // 2, 4), shard // 8, lax.rem(shard, 2)


def gather_kernel(
    cells, w_cell, w_mix, pairs, live, sa, sb, sa_mix, sb_mix, plist, stage, cell_w, mix_w,
    ids, send_sem, recv_sem, local_sem
):
    columns, samples, features = stage.shape
    x, y, z, core = place()
    shard = lambda z_, y_, c_: z_ * 8 + y_ * 2 + c_
    xr, xl = lax.rem(x + 1, 4), lax.rem(x + 3, 4)
    yr, yl, yo = lax.rem(y + 1, 4), lax.rem(y + 3, 4), lax.rem(y + 2, 4)
    zs = [lax.rem(z + k, 8) for k in range(8)]
    me = shard(z, y, core)
    dev = {
        "x+": (xr, me),
        "x-": (xl, me),
        "y+": (x, shard(z, yr, core)),
        "y-": (x, shard(z, yl, core)),
        "z+": (x, shard(zs[1], y, core)),
        "z-": (x, shard(zs[7], y, core)),
        "c": (x, shard(z, y, 1 - core)),
    }
    barrier = pltpu.get_barrier_semaphore()
    for d in dev.values():
        pl.semaphore_signal(barrier, inc=1, device_id=d, device_id_type=MESH)

    quarter_at = lambda k: pl.ds(4 * lax.rem(x + k, 4), 4)
    thirds = range(0, features, 256)
    moves = [(pairs, ids), (cells.at[quarter_at(0)], stage.at[quarter_at(0)])]
    moves += [(w_cell.at[:, pl.ds(f, 256)], cell_w.at[:, pl.ds(f, 256)]) for f in thirds]
    moves += [(cells.at[quarter_at(k)], stage.at[quarter_at(k)]) for k in (1, 2, 3)]
    moves += [(w_mix, mix_w)]
    loads = [
        pltpu.make_async_copy(src, dst, local_sem.at[k]) for k, (src, dst) in enumerate(moves)
    ]
    for copy in loads:
        copy.start()

    loads[0].wait()
    first_id, second_id = ids[pl.ds(0, 1)], ids[pl.ds(1, 1)]
    slot = lax.broadcasted_iota(jnp.int32, first_id.shape, 1)
    row = jnp.where(slot < live[0], y * 16 + (first_id & 15) + 64 * second_id, -1)
    row = jnp.concatenate([row, jnp.full(row.shape, -1, jnp.int32)], axis=1)
    plist[x, y] = jnp.where(lax.rem(y, 2) == 0, row, pltpu.roll(row, 64, 1))

    def project(k):
        quarter = lax.rem(x + k, 4)
        loads[1 if k == 0 else 4 + k].wait()
        rows = stage[pl.ds(quarter * 4, 4)].reshape(4 * samples, features)
        for third, first in enumerate(thirds):
            if k == 0:
                loads[2 + third].wait()
            block = jnp.dot(
                rows, cell_w[:, pl.ds(first, 256)], preferred_element_type=jnp.float32
            ).astype(jnp.bfloat16)
            sa[pl.ds(y * 16 + quarter * 4, 4), :, pl.ds(first, 256)] = block.reshape(4, samples, 256)

    project(0)
    sb[pl.ds(z * 8 + core * 4, 4)] = sa[pl.ds(y * 16 + 4 * x, 4)]
    pl.semaphore_wait(barrier, len(dev))

    def times_mix(source, result, runs):
        rows = jnp.concatenate([source[pl.ds(*run)] for run in runs], axis=0)
        rows = rows.reshape(-1, features)
        for first in range(0, features, 256):
            block = jnp.dot(
                rows, mix_w[:, pl.ds(first, 256)], preferred_element_type=jnp.float32
            ).astype(jnp.bfloat16).reshape(-1, samples, 256)
            at = 0
            for start, size in runs:
                result[pl.ds(start, size), :, pl.ds(first, 256)] = block[at : at + size]
                at += size

    def mix_a(first_y, step_y, count, half):
        def body(k, carry):
            base = lax.rem(first_y + step_y * k, 4) * 16 + 2 * half
            times_mix(sa, sa_mix, [(base + 4 * q, 2) for q in range(4)])
            return carry
        lax.fori_loop(0, count, body, 0)

    def mix_b(d):
        def body(k, carry):
            times_mix(sb, sb_mix, [(lax.rem(z + 8 - d + 2 * d * k, 8) * 8, 8)])
            return carry
        lax.fori_loop(0, 1 if d == 0 else 2, body, 0)

    def mix_far(c_):
        times_mix(sb, sb_mix, [(zs[4] * 8 + c_ * 4, 4)])

    kinds = {}
    sent = []

    def index_of(kind):
        return kinds.setdefault(kind, len(kinds))

    def send(kind, src, dst, to):
        k = index_of(kind)
        copy = pltpu.make_async_remote_copy(
            src_ref=src, dst_ref=dst, send_sem=send_sem.at[k], recv_sem=recv_sem.at[k],
            device_id=dev[to], device_id_type=MESH,
        )
        copy.start()
        sent.append(copy)

    def arrive(kind, slot, to):
        k = index_of(kind)
        pltpu.make_async_remote_copy(
            src_ref=slot, dst_ref=slot, send_sem=send_sem.at[k], recv_sem=recv_sem.at[k],
            device_id=dev[to], device_id_type=MESH,
        ).wait_recv()

    def a_cols(y_, first, size):
        return sa.at[pl.ds(y_ * 16 + first, size)]

    def b_cols(z_, c_, first, size):
        return sb.at[pl.ds(z_ * 8 + c_ * 4 + first, size)]

    def direct(y_, k):
        return a_cols(y_, 4 * lax.rem(x + k, 4) + 2, 2)

    def last(y_, k):
        return a_cols(y_, 4 * lax.rem(x + k, 4) + 3, 1)

    shared = a_cols(y, 4 * x, 2)
    send("l+", plist.at[x, y], plist.at[x, y], "y+")
    send("l-", plist.at[x, y], plist.at[x, y], "y-")
    for p in (0, 1):
        send(f"z+0{p}", b_cols(z, core, 2 * p, 2), b_cols(z, core, 2 * p, 2), "z+")
        send(f"z-0{p}", b_cols(z, core, 2 * (1 - p), 2), b_cols(z, core, 2 * (1 - p), 2), "z-")
        if p == 0:
            send("y+S", shared, shared, "y+")
            send("y-S", shared, shared, "y-")
    send("y+D0", direct(y, 0), direct(y, 0), "y+")
    send("y-D0", direct(y, 0), direct(y, 0), "y-")
    send("c0", b_cols(z, core, 0, 4), b_cols(z, core, 0, 4), "c")
    project(1)
    send("y-D1", direct(y, 1), direct(y, 1), "y-")
    project(2)
    project(3)
    loads[8].wait()
    other = 1 - core
    arrive_c0 = lambda: arrive("c0", b_cols(z, other, 0, 4), "c")

    def arrive_c(d, p):
        arrive(f"c+{d}{p}", b_cols(zs[8 - d], other, 2 * p, 2), "c")
        arrive(f"c-{d}{p}", b_cols(zs[d], other, 2 * (1 - p), 2), "c")

    def z_round(d, p):
        up = b_cols(zs[8 - d], core, 2 * p, 2)
        down = b_cols(zs[d], core, 2 * (1 - p), 2)
        arrive(f"z+{d - 1}{p}", up, "z-")
        if d < 3 or (d == 3 and p == 0):
            send(f"z+{d}{p}", up, up, "z+")
        send(f"c+{d}{p}", up, up, "c")
        arrive(f"z-{d - 1}{p}", down, "z+")
        if d < 3 or (d == 3 and p == 0):
            send(f"z-{d}{p}", down, down, "z-")
        send(f"c-{d}{p}", down, down, "c")

    mix_a(y, 0, 1, 0)
    mix_a(y, 0, 1, 1)
    arrive_c0()
    mix_b(0)

    below, above = a_cols(yl, 4 * x, 2), a_cols(yr, 4 * x, 2)
    arrive("l+", plist.at[x, yl], "y-")
    send("l+2", plist.at[x, yl], plist.at[x, yl], "y+")
    arrive("l-", plist.at[x, yr], "y+")
    arrive("y+S", below, "y-")
    send("y+S2", below, below, "y+")
    send("x+b", below, below, "x+")
    send("x-b", below, below, "x-")
    arrive("y-S", above, "y+")
    send("x+a", above, above, "x+")
    send("x-a", above, above, "x-")
    z_round(1, 0)

    arrive("y+D0", direct(yl, 0), "y-")
    send("y+c", a_cols(yl, 4 * x + 2, 1), a_cols(yl, 4 * x + 2, 1), "y+")
    for k in (1, 2, 3):
        send(f"y+D{k}", direct(y, k), direct(y, k), "y+")
    arrive("y-D0", direct(yr, 0), "y+")
    send("y-r0", last(yr, 0), last(yr, 0), "y-")
    send("y-D2", direct(y, 2), direct(y, 2), "y-")
    z_round(1, 1)
    arrive("l+2", plist.at[x, yo], "y-")
    send("lx+", plist.at[x], plist.at[x], "x+")
    send("lx-", plist.at[x], plist.at[x], "x-")
    arrive_c(1, 0)
    arrive_c(1, 1)
    mix_b(1)

    arrive("y+S2", a_cols(yo, 4 * x, 2), "y-")
    for j in (0, 1):
        one, two = a_cols(yo, 4 * x + j, 1), a_cols(yo, 4 * x + 1 - j, 1)
        send(f"x+f{j}", one, one, "x+")
        send(f"x-f{1 - j}", two, two, "x-")
    z_round(2, 0)
    got = a_cols(yl, 4 * xl, 2)
    arrive("x+b", got, "x-")
    send("x+b2", got, got, "x+")
    arrive("y-D1", direct(yr, 1), "y+")
    send("y-r1", last(yr, 1), last(yr, 1), "y-")
    send("y-D3", direct(y, 3), direct(y, 3), "y-")
    got = a_cols(yr, 4 * xr, 2)
    arrive("x-a", got, "x+")
    send("x-a2", got, got, "x-")
    arrive("lx+", plist.at[xl], "x-")
    send("lx+2", plist.at[xl], plist.at[xl], "x+")
    arrive("y+c", a_cols(yo, 4 * x + 2, 1), "y-")
    for to in ("x+", "x-"):
        send(to + "c", a_cols(yo, 4 * x + 2, 1), a_cols(yo, 4 * x + 2, 1), to)
    z_round(2, 1)

    arrive_c(2, 0)
    arrive_c(2, 1)
    mix_b(2)
    early = len(sent)
    arrive("y-D2", direct(yr, 2), "y+")
    send("y-r2", last(yr, 2), last(yr, 2), "y-")
    got = a_cols(yo, 4 * xl, 1)
    arrive("x+f0", got, "x-")
    send("x+f02", got, got, "x+")
    got = a_cols(yo, 4 * xr + 1, 1)
    arrive("x-f1", got, "x+")
    send("x-f12", got, got, "x-")
    z_round(3, 0)
    xo = lax.rem(x + 2, 4)
    arrive("x-b", a_cols(yl, 4 * xr, 2), "x+")
    arrive("x+a", a_cols(yr, 4 * xl, 2), "x-")
    arrive("x+b2", a_cols(yl, 4 * xo, 2), "x-")
    arrive("x-a2", a_cols(yr, 4 * xo, 2), "x+")
    mix_a(yl, 2, 2, 0)
    got = a_cols(yo, 4 * xl + 2, 1)
    arrive("x+c", got, "x-")
    send("x+c2", got, got, "x+")
    z_round(3, 1)
    arrive("y-D3", direct(yr, 3), "y+")
    send("y-r3", last(yr, 3), last(yr, 3), "y-")
    mix_a(yr, 0, 1, 1)
    arrive_c(3, 0)
    arrive_c(3, 1)
    mix_b(3)
    for k in (1, 2, 3):
        arrive(f"y+D{k}", direct(yl, k), "y-")
    mix_a(yl, 0, 1, 1)
    arrive("x+f1", a_cols(yo, 4 * xl + 1, 1), "x-")
    arrive("x-f0", a_cols(yo, 4 * xr, 1), "x+")
    arrive("x+f02", a_cols(yo, 4 * xo, 1), "x-")
    arrive("x-f12", a_cols(yo, 4 * xo + 1, 1), "x+")
    mix_a(yo, 0, 1, 0)
    arrive("lx-", plist.at[xr], "x+")
    arrive("lx+2", plist.at[xo], "x-")
    for copy in sent[:early]:
        copy.wait_send()

    z_round(4, 0)
    arrive("x-c", a_cols(yo, 4 * xr + 2, 1), "x+")
    arrive("x+c2", a_cols(yo, 4 * xo + 2, 1), "x-")
    for k in range(4):
        arrive(f"y-r{k}", last(yo, k), "y+")
    mix_a(yo, 0, 1, 1)
    mix_far(core)
    for copy in sent[early:-2]:
        copy.wait_send()
    arrive_c(4, 0)
    mix_far(other)
    sent[:-2] = []
    for copy in sent:
        copy.wait_send()
    assert len(kinds) <= COPIES


COPIES = 96


def gather_blocks(cells, w_cell, w_mix, pairs, counts):
    vmem = pl.BlockSpec(memory_space=pltpu.VMEM)
    columns, samples, features = cells.shape
    blocks = pltpu.VMEM((64, samples, features), jnp.bfloat16)
    return pl.pallas_call(
        gather_kernel,
        out_shape=(blocks,) * 4 + (pltpu.VMEM((4, 4, 1, 128), jnp.int32),),
        in_specs=[pl.BlockSpec(memory_space=pltpu.HBM)] * 4 + [pl.BlockSpec(memory_space=pltpu.SMEM)],
        out_specs=(vmem,) * 5,
        scratch_shapes=[
            pltpu.VMEM((columns, samples, features), jnp.bfloat16),
            pltpu.VMEM(w_cell.shape, jnp.bfloat16),
            pltpu.VMEM(w_mix.shape, jnp.bfloat16),
            pltpu.VMEM(pairs.shape, jnp.int32),
            pltpu.SemaphoreType.DMA((COPIES,)),
            pltpu.SemaphoreType.DMA((COPIES,)),
            pltpu.SemaphoreType.DMA((9,)),
        ],
        compiler_params=pltpu.CompilerParams(
            collective_id=0, has_side_effects=True, vmem_limit_bytes=12 << 20
        ),
        name="gather_blocks",
    )(cells, w_cell, w_mix, pairs, counts)


def score_kernel(
    sa, sb, sa_mix, sb_mix, plist, w_pool, out,
    pool_w, raw, blend, pooled, target, table, lst, sem, list_sem
):
    samples, features = sa.shape[1:]
    scale = 1.0 / math.sqrt(features)
    load = pltpu.make_async_copy(w_pool, pool_w, sem)
    load.start()

    x, y, _, _ = place()
    codes = jnp.concatenate(
        [jnp.maximum(plist[k // 2, k % 2 * 2], plist[k // 2, k % 2 * 2 + 1]) for k in range(8)],
        axis=0,
    )
    b_id = codes >> 6
    mine = (codes >= 0) & (((b_id >> 5) & 3) == y) & (((b_id >> 2) & 3) == x)
    flag = jnp.where(mine, 1.0, 0.0)
    row_id = lax.broadcasted_iota(jnp.int32, (8, 128), 0)
    lane = lambda n: lax.broadcasted_iota(jnp.int32, (128, n), 1)
    upto = jnp.where(lax.broadcasted_iota(jnp.int32, (128, 128), 0) < lane(128), 1.0, 0.0)
    ahead = jnp.dot(
        flag.astype(jnp.bfloat16), upto.astype(jnp.bfloat16), preferred_element_type=jnp.float32
    )
    rows_upto = jnp.broadcast_to(jnp.sum(flag, axis=1, keepdims=True), (8, 128))
    own = rows_upto
    for shift in (1, 2, 4):
        rows_upto = rows_upto + jnp.where(
            row_id >= shift, pltpu.roll(rows_upto, shift, 0), 0.0
        )
    position = jnp.where(mine, (ahead + rows_upto - own).astype(jnp.int32), -1)
    target[...] = jnp.where(
        mine, 8 * (position >> 2) + 4 * ((position >> 1) & 1) + 2 + (position & 1), -1
    )
    spread = position.T
    a_at = (codes & 63).astype(jnp.bfloat16)
    b_at = ((b_id >> 7) * 8 + ((b_id >> 4) & 1) * 4 + (b_id & 3)).astype(jnp.bfloat16)
    found_a = jnp.zeros((8, CAPACITY), jnp.float32)
    found_b = jnp.zeros((8, CAPACITY), jnp.float32)
    for k in range(8):
        hit = jnp.where(spread[:, k : k + 1] == lane(CAPACITY), 1.0, 0.0).astype(jnp.bfloat16)
        keep = row_id == k
        both = jnp.concatenate(
            [jnp.where(keep, a_at, 0), jnp.where(keep, b_at, 0)], axis=0
        ).astype(jnp.bfloat16)
        got = jnp.dot(both, hit, preferred_element_type=jnp.float32)
        found_a = found_a + got[:8]
        found_b = found_b + got[8:]
    sum_rows = lambda v: jnp.sum(v, axis=0, keepdims=True).astype(jnp.int32)
    total = jnp.broadcast_to(rows_upto[7:, :1], (1, CAPACITY)).astype(jnp.int32)
    table[0] = sum_rows(found_a)
    table[1] = sum_rows(found_b)
    table[2] = total
    move = pltpu.make_async_copy(table, lst, list_sem)
    move.start()
    move.wait()
    count = lst[2, 0, 0]
    steps = (count + GROUP - 1) // GROUP

    two = 2 * samples
    same = (
        lax.broadcasted_iota(jnp.int32, (two, two), 0) // samples
        == lax.broadcasted_iota(jnp.int32, (two, two), 1) // samples
    )
    identity = jnp.where(
        lax.broadcasted_iota(jnp.int32, (two, two), 0) == lax.broadcasted_iota(jnp.int32, (two, two), 1),
        1.0, 0.0,
    ).astype(jnp.bfloat16)
    for h in range(GROUP // 2):
        blend[h, pl.ds(0, two), pl.ds(0, two)] = identity
        blend[h, pl.ds(two, two), pl.ds(two, two)] = identity

    def pair_rows(source, which, step, h):
        first = step * GROUP + 2 * h
        return jnp.concatenate(
            [source[lst[which, 0, first]], source[lst[which, 0, first + 1]]], axis=0
        )

    def scores(step, h):
        found = lax.dot_general(
            pair_rows(sa, 0, step, h), pair_rows(sb, 1, step, h), (((1,), (1,)), ((), ())),
            preferred_element_type=jnp.float32,
        )
        return jnp.where(same, found * scale, -1e30)

    def attend(found, axis):
        weight = jnp.exp(found - jnp.max(found, axis=axis, keepdims=True))
        return weight * (1.0 / jnp.sum(weight, axis=axis, keepdims=True))

    def keep_weights(found, h):
        blend[h, pl.ds(0, two), pl.ds(two, two)] = attend(found, 1).astype(jnp.bfloat16)
        blend[h, pl.ds(two, two), pl.ds(0, two)] = attend(found, 0).T.astype(jnp.bfloat16)

    def pool(step):
        products = [
            jnp.concatenate(
                [pair_rows(sa_mix, 0, step, h), pair_rows(sb_mix, 1, step, h)], axis=0
            )
            for h in range(GROUP // 2)
        ]
        row = pl.multiple_of(step * 2 * GROUP, 2 * GROUP)
        for first in range(0, features, 256):
            means = []
            for h in range(GROUP // 2):
                hidden = jnp.tanh(
                    jnp.dot(
                        blend[h], products[h][:, first : first + 256],
                        preferred_element_type=jnp.float32,
                    )
                )
                means.append(jnp.sum(hidden.reshape(4, samples, 256), axis=1) * (1.0 / samples))
            pooled[pl.ds(row, 2 * GROUP), pl.ds(first, 256)] = jnp.concatenate(means, axis=0)

    halves = range(GROUP // 2)

    def keep_scores(step):
        for h in halves:
            raw[h] = scores(step, h)

    def step_body(step, carry):
        now = [raw[h] for h in halves]
        pool(step - 1)
        for h in halves:
            keep_weights(now[h], h)
        keep_scores(jnp.minimum(step + 1, steps - 1))
        return carry

    @pl.when(steps > 0)
    def _():
        keep_scores(0)
        for h in halves:
            keep_weights(raw[h], h)
        keep_scores(jnp.minimum(1, steps - 1))
        lax.fori_loop(1, steps, step_body, 0)
        pool(steps - 1)

    load.wait()
    out[...] = jnp.zeros_like(out)

    def finish(chunk, carry):
        row = pl.multiple_of(chunk * 256, 256)
        vectors = pooled[pl.ds(row, 256)].astype(jnp.bfloat16)
        right = jnp.dot(vectors, pool_w[...], preferred_element_type=jnp.float32)
        left = pltpu.roll(right, 2, 0)
        inner = jnp.mean(left * right, axis=-1, keepdims=True)
        size = jnp.mean(right * right, axis=-1, keepdims=True) + EPSILON
        norms = size * pltpu.roll(size, 2, 0)
        score = inner / jnp.sqrt(norms) / SOFTMAX_WARMTH
        number = row + lax.broadcasted_iota(jnp.int32, (256, 128), 0)
        for k in range(8):
            hit = target[pl.ds(k, 1)] == number
            out[k] += jnp.sum(jnp.where(hit, score, 0.0), axis=0, keepdims=True)
        return carry

    lax.fori_loop(0, (steps + 31) // 32, finish, 0)


def score_pairs(sa, sb, sa_mix, sb_mix, plist, w_pool):
    samples, features = sa.shape[1:]
    vmem = pl.BlockSpec(memory_space=pltpu.VMEM)
    two = 2 * samples
    return pl.pallas_call(
        score_kernel,
        out_shape=pltpu.VMEM((8, 1, 128), jnp.float32),
        in_specs=[vmem] * 5 + [pl.BlockSpec(memory_space=pltpu.HBM)],
        out_specs=vmem,
        scratch_shapes=[
            pltpu.VMEM(w_pool.shape, jnp.bfloat16),
            pltpu.VMEM((GROUP // 2, two, two), jnp.float32),
            pltpu.VMEM((GROUP // 2, 2 * two, 2 * two), jnp.bfloat16),
            pltpu.VMEM((2 * CAPACITY, features), jnp.float32),
            pltpu.VMEM((8, 128), jnp.int32),
            pltpu.VMEM((3, 1, CAPACITY), jnp.int32),
            pltpu.SMEM((3, 1, CAPACITY), jnp.int32),
            pltpu.SemaphoreType.DMA,
            pltpu.SemaphoreType.DMA,
        ],
        compiler_params=pltpu.CompilerParams(vmem_limit_bytes=16 << 20),
        name="score_pairs",
    )(sa, sb, sa_mix, sb_mix, plist, w_pool)


def return_kernel(part, out, landed, send_sem, recv_sem):
    x, y, z, core = place()
    me = z * 8 + y * 2 + core

    def partner(k):
        return lax.rem(x + k // 4, 4), lax.rem(y + k % 4, 4)

    barrier = pltpu.get_barrier_semaphore()
    for k in range(1, 16):
        tx, ty = partner(k)
        pl.semaphore_signal(
            barrier, inc=1, device_id=(tx, z * 8 + ty * 2 + core), device_id_type=MESH
        )
    pl.semaphore_wait(barrier, 15)
    sent = []
    for k in range(1, 16):
        tx, ty = partner(k)
        copy = pltpu.make_async_remote_copy(
            src_ref=part.at[tx * 2 + ty // 2], dst_ref=landed.at[k],
            send_sem=send_sem.at[k], recv_sem=recv_sem.at[k],
            device_id=(tx, z * 8 + ty * 2 + core), device_id_type=MESH,
        )
        copy.start()
        sent.append(copy)
    total = part[x * 2 + y // 2]
    for k, copy in enumerate(sent, start=1):
        copy.wait_recv()
        total = total + landed[k]
    half = jnp.where(lax.rem(y, 2) == 0, total, pltpu.roll(total, 64, 1))
    out[...] = half[:, :64]
    for copy in sent:
        copy.wait_send()


def return_scores(part):
    vmem = pl.BlockSpec(memory_space=pltpu.VMEM)
    return pl.pallas_call(
        return_kernel,
        out_shape=jax.ShapeDtypeStruct((1, 64), jnp.float32),
        in_specs=[vmem],
        out_specs=vmem,
        scratch_shapes=[
            pltpu.VMEM((16, 1, 128), jnp.float32),
            pltpu.SemaphoreType.DMA((16,)),
            pltpu.SemaphoreType.DMA((16,)),
        ],
        compiler_params=pltpu.CompilerParams(
            collective_id=1, has_side_effects=True, vmem_limit_bytes=1 << 20
        ),
        name="return_scores",
    )(part)


def local(cells, w_cell, w_mix, w_pool, pairs, counts):
    in_place = lambda v: pltpu.with_memory_space_constraint(v, pltpu.HBM)
    cells, w_cell, w_mix, w_pool = map(in_place, (cells, w_cell, w_mix, w_pool))
    blocks = gather_blocks(cells, w_cell, w_mix, in_place(pairs.T), counts)
    return return_scores(score_pairs(*blocks, w_pool)).reshape(pairs.shape[0])


def solution(mesh):
    placed = (P("shard", None, None), P(), P(), P(), P(("grp", "shard"), None), P(("grp", "shard")))
    return jax.shard_map(
        local, mesh=mesh, in_specs=placed, out_specs=P(("grp", "shard")), check_vma=False
    )
```

```python
import functools
import math

import jax
import jax.numpy as jnp
from jax import lax
from jax.experimental import pallas as pl
from jax.experimental.pallas import tpu as pltpu
from jax.sharding import PartitionSpec as P

SOFTMAX_WARMTH = 0.07
EPSILON = 1e-06
MESH = pl.DeviceIdType.MESH
CAPACITY = 512
GROUP = 4


def place():
    x = lax.axis_index("grp")
    shard = lax.axis_index("shard")
    return x, lax.rem(shard // 2, 4), shard // 8, lax.rem(shard, 2)


def gather_kernel(
    cells, w_cell, w_mix, pairs, live, sa, sb, sa_mix, sb_mix, plist, stage, cell_w, mix_w,
    ids, send_sem, recv_sem, local_sem
):
    columns, samples, features = stage.shape
    x, y, z, core = place()
    quarter_at = lambda k: pl.ds(4 * lax.rem(x + k, 4), 4)
    thirds = range(0, features, 256)
    moves = [(pairs, ids), (cells.at[quarter_at(0)], stage.at[quarter_at(0)])]
    moves += [(w_cell.at[:, pl.ds(f, 256)], cell_w.at[:, pl.ds(f, 256)]) for f in thirds]
    moves += [(cells.at[quarter_at(k)], stage.at[quarter_at(k)]) for k in (1, 2, 3)]
    moves += [(w_mix, mix_w)]
    loads = [
        pltpu.make_async_copy(src, dst, local_sem.at[k]) for k, (src, dst) in enumerate(moves)
    ]
    for copy in loads:
        copy.start()

    shard = lambda z_, y_, c_: z_ * 8 + y_ * 2 + c_
    xr, xl = lax.rem(x + 1, 4), lax.rem(x + 3, 4)
    yr, yl, yo = lax.rem(y + 1, 4), lax.rem(y + 3, 4), lax.rem(y + 2, 4)
    zs = [lax.rem(z + k, 8) for k in range(8)]
    me = shard(z, y, core)
    dev = {
        "x+": (xr, me),
        "x-": (xl, me),
        "y+": (x, shard(z, yr, core)),
        "y-": (x, shard(z, yl, core)),
        "z+": (x, shard(zs[1], y, core)),
        "z-": (x, shard(zs[7], y, core)),
        "c": (x, shard(z, y, 1 - core)),
    }
    barrier = pltpu.get_barrier_semaphore()
    for d in dev.values():
        pl.semaphore_signal(barrier, inc=1, device_id=d, device_id_type=MESH)

    def project(k):
        quarter = lax.rem(x + k, 4)
        loads[1 if k == 0 else 4 + k].wait()
        rows = stage[pl.ds(quarter * 4, 4)].reshape(4 * samples, features)
        for third, first in enumerate(thirds):
            if k == 0:
                loads[2 + third].wait()
            block = jnp.dot(
                rows, cell_w[:, pl.ds(first, 256)], preferred_element_type=jnp.float32
            ).astype(jnp.bfloat16)
            sa[pl.ds(y * 16 + quarter * 4, 4), :, pl.ds(first, 256)] = block.reshape(4, samples, 256)

    project(0)
    sb[pl.ds(z * 8 + core * 4, 4)] = sa[pl.ds(y * 16 + 4 * x, 4)]
    loads[0].wait()
    first_id, second_id = ids[pl.ds(0, 1)], ids[pl.ds(1, 1)]
    slot = lax.broadcasted_iota(jnp.int32, first_id.shape, 1)
    row = jnp.where(slot < live[0], y * 16 + (first_id & 15) + 64 * second_id, -1)
    row = jnp.concatenate([row, jnp.full(row.shape, -1, jnp.int32)], axis=1)
    plist[x, y] = jnp.where(lax.rem(y, 2) == 0, row, pltpu.roll(row, 64, 1))

    pl.semaphore_wait(barrier, len(dev))

    kinds = {}
    sent = []

    def index_of(kind):
        return kinds.setdefault(kind, len(kinds))

    def send(kind, src, dst, to):
        k = index_of(kind)
        copy = pltpu.make_async_remote_copy(
            src_ref=src, dst_ref=dst, send_sem=send_sem.at[k], recv_sem=recv_sem.at[k],
            device_id=dev[to], device_id_type=MESH,
        )
        copy.start()
        sent.append(copy)

    def arrive(kind, slot, to):
        k = index_of(kind)
        pltpu.make_async_remote_copy(
            src_ref=slot, dst_ref=slot, send_sem=send_sem.at[k], recv_sem=recv_sem.at[k],
            device_id=dev[to], device_id_type=MESH,
        ).wait_recv()

    def a_cols(y_, first, size):
        return sa.at[pl.ds(y_ * 16 + first, size)]

    def b_cols(z_, c_, first, size):
        return sb.at[pl.ds(z_ * 8 + c_ * 4 + first, size)]

    def times_mix(*runs):
        rows = jnp.concatenate([source[pl.ds(at, size)] for source, _, at, size in runs], axis=0)
        rows = rows.reshape(-1, features)
        for first in thirds:
            block = jnp.dot(
                rows, mix_w[:, pl.ds(first, 256)], preferred_element_type=jnp.float32
            ).astype(jnp.bfloat16).reshape(-1, samples, 256)
            done = 0
            for _, result, at, size in runs:
                result[pl.ds(at, size), :, pl.ds(first, 256)] = block[done : done + size]
                done += size

    def some_a(y_, half):
        return [(sa, sa_mix, y_ * 16 + 2 * half + 4 * q, 2) for q in range(4)]

    def some_b(z_, c_):
        return [(sb, sb_mix, z_ * 8 + c_ * 4, 4)]

    def own_b(d):
        return some_b(zs[8 - d], core) + some_b(zs[d], core)

    def products(z_, c_):
        return sb_mix.at[pl.ds(z_ * 8 + c_ * 4, 4)]

    def send_products(d):
        for sign, z_ in (("+", zs[8 - d]), ("-", zs[d])):
            send(f"m{sign}{d}", products(z_, core), products(z_, core), "c")

    def direct(y_, k):
        return a_cols(y_, 4 * lax.rem(x + k, 4) + 2, 2)

    def last(y_, k):
        return a_cols(y_, 4 * lax.rem(x + k, 4) + 3, 1)

    shared = a_cols(y, 4 * x, 2)
    for p in (0, 1):
        send(f"z+0{p}", b_cols(z, core, 2 * p, 2), b_cols(z, core, 2 * p, 2), "z+")
        send(f"z-0{p}", b_cols(z, core, 2 * (1 - p), 2), b_cols(z, core, 2 * (1 - p), 2), "z-")
        if p == 0:
            send("y+S", shared, shared, "y+")
            send("y-S", shared, shared, "y-")
    send("l+", plist.at[x, y], plist.at[x, y], "y+")
    send("l-", plist.at[x, y], plist.at[x, y], "y-")
    send("y+D0", direct(y, 0), direct(y, 0), "y+")
    send("y-D0", direct(y, 0), direct(y, 0), "y-")
    send("c0", b_cols(z, core, 0, 4), b_cols(z, core, 0, 4), "c")
    project(1)
    send("y-D1", direct(y, 1), direct(y, 1), "y-")
    project(2)
    project(3)
    loads[8].wait()
    other = 1 - core
    arrive_c0 = lambda: arrive("c0", b_cols(z, other, 0, 4), "c")

    def arrive_c(d, p):
        arrive(f"c+{d}{p}", b_cols(zs[8 - d], other, 2 * p, 2), "c")
        arrive(f"c-{d}{p}", b_cols(zs[d], other, 2 * (1 - p), 2), "c")

    def z_round(d, p):
        up = b_cols(zs[8 - d], core, 2 * p, 2)
        down = b_cols(zs[d], core, 2 * (1 - p), 2)
        arrive(f"z+{d - 1}{p}", up, "z-")
        if d < 3 or (d == 3 and p == 0):
            send(f"z+{d}{p}", up, up, "z+")
        send(f"c+{d}{p}", up, up, "c")
        arrive(f"z-{d - 1}{p}", down, "z+")
        if d < 3 or (d == 3 and p == 0):
            send(f"z-{d}{p}", down, down, "z-")
        send(f"c-{d}{p}", down, down, "c")

    times_mix(*some_b(z, core), *some_a(y, 0))
    times_mix(*some_a(y, 1))
    send("m0", products(z, core), products(z, core), "c")

    below, above = a_cols(yl, 4 * x, 2), a_cols(yr, 4 * x, 2)
    arrive("y+S", below, "y-")
    send("y+S2", below, below, "y+")
    send("x+b", below, below, "x+")
    send("x-b", below, below, "x-")
    arrive("y-S", above, "y+")
    send("x+a", above, above, "x+")
    send("x-a", above, above, "x-")
    arrive("l+", plist.at[x, yl], "y-")
    send("l+2", plist.at[x, yl], plist.at[x, yl], "y+")
    arrive("l-", plist.at[x, yr], "y+")
    z_round(1, 0)

    arrive("y+D0", direct(yl, 0), "y-")
    send("y+c", a_cols(yl, 4 * x + 2, 1), a_cols(yl, 4 * x + 2, 1), "y+")
    for k in (1, 2, 3):
        send(f"y+D{k}", direct(y, k), direct(y, k), "y+")
    arrive("y-D0", direct(yr, 0), "y+")
    send("y-r0", last(yr, 0), last(yr, 0), "y-")
    send("y-D2", direct(y, 2), direct(y, 2), "y-")
    z_round(1, 1)
    arrive("l+2", plist.at[x, yo], "y-")
    send("lx+", plist.at[x], plist.at[x], "x+")
    send("lx-", plist.at[x], plist.at[x], "x-")
    times_mix(*own_b(1))

    arrive("y+S2", a_cols(yo, 4 * x, 2), "y-")
    for j in (0, 1):
        one, two = a_cols(yo, 4 * x + j, 1), a_cols(yo, 4 * x + 1 - j, 1)
        send(f"x+f{j}", one, one, "x+")
        send(f"x-f{1 - j}", two, two, "x-")
    z_round(2, 0)
    got = a_cols(yl, 4 * xl, 2)
    arrive("x+b", got, "x-")
    send("x+b2", got, got, "x+")
    arrive("y-D1", direct(yr, 1), "y+")
    send("y-r1", last(yr, 1), last(yr, 1), "y-")
    send("y-D3", direct(y, 3), direct(y, 3), "y-")
    got = a_cols(yr, 4 * xr, 2)
    arrive("x-a", got, "x+")
    send("x-a2", got, got, "x-")
    arrive("lx+", plist.at[xl], "x-")
    send("lx+2", plist.at[xl], plist.at[xl], "x+")
    arrive("y+c", a_cols(yo, 4 * x + 2, 1), "y-")
    for to in ("x+", "x-"):
        send(to + "c", a_cols(yo, 4 * x + 2, 1), a_cols(yo, 4 * x + 2, 1), to)
    z_round(2, 1)

    times_mix(*own_b(2))
    send_products(1)
    early = len(sent)
    arrive("y-D2", direct(yr, 2), "y+")
    send("y-r2", last(yr, 2), last(yr, 2), "y-")
    got = a_cols(yo, 4 * xl, 1)
    arrive("x+f0", got, "x-")
    send("x+f02", got, got, "x+")
    got = a_cols(yo, 4 * xr + 1, 1)
    arrive("x-f1", got, "x+")
    send("x-f12", got, got, "x-")
    z_round(3, 0)
    xo = lax.rem(x + 2, 4)
    arrive("x-b", a_cols(yl, 4 * xr, 2), "x+")
    arrive("x+a", a_cols(yr, 4 * xl, 2), "x-")
    arrive("x+b2", a_cols(yl, 4 * xo, 2), "x-")
    arrive("x-a2", a_cols(yr, 4 * xo, 2), "x+")
    for far_y in (yl, yr):
        times_mix(*some_a(far_y, 0))
    send_products(2)
    got = a_cols(yo, 4 * xl + 2, 1)
    arrive("x+c", got, "x-")
    send("x+c2", got, got, "x+")
    z_round(3, 1)
    arrive("y-D3", direct(yr, 3), "y+")
    send("y-r3", last(yr, 3), last(yr, 3), "y-")
    times_mix(*some_a(yr, 1), *own_b(3))
    send_products(3)
    for copy in sent[:early]:
        copy.wait_send()
    late = sent[early:]

    z_round(4, 0)
    arrive("x-c", a_cols(yo, 4 * xr + 2, 1), "x+")
    arrive("x+c2", a_cols(yo, 4 * xo + 2, 1), "x-")
    for k in range(4):
        arrive(f"y-r{k}", last(yo, k), "y+")
    for k in (1, 2, 3):
        arrive(f"y+D{k}", direct(yl, k), "y-")
    arrive("x+f1", a_cols(yo, 4 * xl + 1, 1), "x-")
    arrive("x-f0", a_cols(yo, 4 * xr, 1), "x+")
    arrive("x+f02", a_cols(yo, 4 * xo, 1), "x-")
    arrive("x-f12", a_cols(yo, 4 * xo + 1, 1), "x+")
    times_mix(*some_a(yl, 1), *some_a(yo, 0), *some_a(yo, 1), *some_b(zs[4], core))
    for copy in late:
        copy.wait_send()
    arrive("lx-", plist.at[xr], "x+")
    arrive("lx+2", plist.at[xo], "x-")
    arrive_c0()
    arrive("m0", products(z, other), "c")
    for d in (1, 2, 3):
        arrive_c(d, 0)
        arrive_c(d, 1)
        arrive(f"m+{d}", products(zs[8 - d], other), "c")
        arrive(f"m-{d}", products(zs[d], other), "c")
    arrive_c(4, 0)
    times_mix(*some_b(zs[4], other))
    del sent[:-2]
    for copy in sent:
        copy.wait_send()
    assert len(kinds) <= COPIES


COPIES = 96


def gather_blocks(cells, w_cell, w_mix, pairs, counts):
    vmem = pl.BlockSpec(memory_space=pltpu.VMEM)
    columns, samples, features = cells.shape
    blocks = pltpu.VMEM((64, samples, features), jnp.bfloat16)
    return pl.pallas_call(
        gather_kernel,
        out_shape=(blocks,) * 4 + (pltpu.VMEM((4, 4, 1, 128), jnp.int32),),
        in_specs=[pl.BlockSpec(memory_space=pltpu.HBM)] * 4 + [pl.BlockSpec(memory_space=pltpu.SMEM)],
        out_specs=(vmem,) * 5,
        scratch_shapes=[
            pltpu.VMEM((columns, samples, features), jnp.bfloat16),
            pltpu.VMEM(w_cell.shape, jnp.bfloat16),
            pltpu.VMEM(w_mix.shape, jnp.bfloat16),
            pltpu.VMEM(pairs.shape, jnp.int32),
            pltpu.SemaphoreType.DMA((COPIES,)),
            pltpu.SemaphoreType.DMA((COPIES,)),
            pltpu.SemaphoreType.DMA((9,)),
        ],
        compiler_params=pltpu.CompilerParams(
            collective_id=0, has_side_effects=True, vmem_limit_bytes=12 << 20
        ),
        name="gather_blocks",
    )(cells, w_cell, w_mix, pairs, counts)


def score_kernel(
    sa, sb, sa_mix, sb_mix, plist, w_pool, out,
    pool_w, raw, blend, pooled, target, table, lst, sem, list_sem
):
    samples, features = sa.shape[1:]
    scale = 1.0 / math.sqrt(features)
    load = pltpu.make_async_copy(w_pool, pool_w, sem)
    load.start()

    x, y, _, _ = place()
    codes = jnp.concatenate(
        [jnp.maximum(plist[k // 2, k % 2 * 2], plist[k // 2, k % 2 * 2 + 1]) for k in range(8)],
        axis=0,
    )
    b_id = codes >> 6
    mine = (codes >= 0) & (((b_id >> 5) & 3) == y) & (((b_id >> 2) & 3) == x)
    flag = jnp.where(mine, 1.0, 0.0)
    row_id = lax.broadcasted_iota(jnp.int32, (8, 128), 0)
    lane = lambda n: lax.broadcasted_iota(jnp.int32, (128, n), 1)
    upto = jnp.where(lax.broadcasted_iota(jnp.int32, (128, 128), 0) < lane(128), 1.0, 0.0)
    ahead = jnp.dot(
        flag.astype(jnp.bfloat16), upto.astype(jnp.bfloat16), preferred_element_type=jnp.float32
    )
    rows_upto = jnp.broadcast_to(jnp.sum(flag, axis=1, keepdims=True), (8, 128))
    own = rows_upto
    for shift in (1, 2, 4):
        rows_upto = rows_upto + jnp.where(
            row_id >= shift, pltpu.roll(rows_upto, shift, 0), 0.0
        )
    position = jnp.where(mine, (ahead + rows_upto - own).astype(jnp.int32), -1)
    target[...] = jnp.where(
        mine, 8 * (position >> 2) + 4 * ((position >> 1) & 1) + 2 + (position & 1), -1
    )
    spread = position.T
    a_at = (codes & 63).astype(jnp.bfloat16)
    b_at = ((b_id >> 7) * 8 + ((b_id >> 4) & 1) * 4 + (b_id & 3)).astype(jnp.bfloat16)
    found_a = jnp.zeros((8, CAPACITY), jnp.float32)
    found_b = jnp.zeros((8, CAPACITY), jnp.float32)
    for k in range(8):
        hit = jnp.where(spread[:, k : k + 1] == lane(CAPACITY), 1.0, 0.0).astype(jnp.bfloat16)
        keep = row_id == k
        both = jnp.concatenate(
            [jnp.where(keep, a_at, 0), jnp.where(keep, b_at, 0)], axis=0
        ).astype(jnp.bfloat16)
        got = jnp.dot(both, hit, preferred_element_type=jnp.float32)
        found_a = found_a + got[:8]
        found_b = found_b + got[8:]
    sum_rows = lambda v: jnp.sum(v, axis=0, keepdims=True).astype(jnp.int32)
    total = jnp.broadcast_to(rows_upto[7:, :1], (1, CAPACITY)).astype(jnp.int32)
    table[0] = sum_rows(found_a)
    table[1] = sum_rows(found_b)
    table[2] = total
    move = pltpu.make_async_copy(table, lst, list_sem)
    move.start()
    move.wait()
    count = lst[2, 0, 0]
    steps = (count + GROUP - 1) // GROUP

    two = 2 * samples
    same = (
        lax.broadcasted_iota(jnp.int32, (two, two), 0) // samples
        == lax.broadcasted_iota(jnp.int32, (two, two), 1) // samples
    )
    identity = jnp.where(
        lax.broadcasted_iota(jnp.int32, (two, two), 0) == lax.broadcasted_iota(jnp.int32, (two, two), 1),
        1.0, 0.0,
    ).astype(jnp.bfloat16)
    for h in range(GROUP // 2):
        blend[h, pl.ds(0, two), pl.ds(0, two)] = identity
        blend[h, pl.ds(two, two), pl.ds(two, two)] = identity

    def pair_rows(source, which, step, h):
        first = step * GROUP + 2 * h
        return jnp.concatenate(
            [source[lst[which, 0, first]], source[lst[which, 0, first + 1]]], axis=0
        )

    def scores(step, h):
        found = lax.dot_general(
            pair_rows(sa, 0, step, h), pair_rows(sb, 1, step, h), (((1,), (1,)), ((), ())),
            preferred_element_type=jnp.float32,
        )
        return jnp.where(same, found * scale, -1e30)

    def attend(found, axis):
        weight = jnp.exp(found - jnp.max(found, axis=axis, keepdims=True))
        return weight * (1.0 / jnp.sum(weight, axis=axis, keepdims=True))

    def keep_weights(found, h):
        blend[h, pl.ds(0, two), pl.ds(two, two)] = attend(found, 1).astype(jnp.bfloat16)
        blend[h, pl.ds(two, two), pl.ds(0, two)] = attend(found, 0).T.astype(jnp.bfloat16)

    def pool(step):
        products = [
            jnp.concatenate(
                [pair_rows(sa_mix, 0, step, h), pair_rows(sb_mix, 1, step, h)], axis=0
            )
            for h in range(GROUP // 2)
        ]
        row = pl.multiple_of(step * 2 * GROUP, 2 * GROUP)
        for first in range(0, features, 256):
            means = []
            for h in range(GROUP // 2):
                hidden = jnp.tanh(
                    jnp.dot(
                        blend[h], products[h][:, first : first + 256],
                        preferred_element_type=jnp.float32,
                    )
                )
                means.append(jnp.sum(hidden.reshape(4, samples, 256), axis=1) * (1.0 / samples))
            pooled[pl.ds(row, 2 * GROUP), pl.ds(first, 256)] = jnp.concatenate(means, axis=0)

    halves = range(GROUP // 2)

    def keep_scores(step):
        for h in halves:
            raw[h] = scores(step, h)

    def one_step(step):
        now = [raw[h] for h in halves]
        pool(step - 1)
        for h in halves:
            keep_weights(now[h], h)
        keep_scores(jnp.minimum(step + 1, steps - 1))

    def two_steps(turn, carry):
        one_step(2 * turn + 1)
        one_step(2 * turn + 2)
        return carry

    @pl.when(steps > 0)
    def _():
        keep_scores(0)
        for h in halves:
            keep_weights(raw[h], h)
        keep_scores(jnp.minimum(1, steps - 1))
        lax.fori_loop(0, (steps - 1) // 2, two_steps, 0)
        pl.when(lax.rem(steps, 2) == 0)(lambda: one_step(steps - 1))
        pool(steps - 1)

    load.wait()
    out[...] = jnp.zeros_like(out)

    def finish(chunk, carry):
        row = pl.multiple_of(chunk * 256, 256)
        vectors = pooled[pl.ds(row, 256)].astype(jnp.bfloat16)
        right = jnp.dot(vectors, pool_w[...], preferred_element_type=jnp.float32)
        left = pltpu.roll(right, 2, 0)
        inner = jnp.mean(left * right, axis=-1, keepdims=True)
        size = jnp.mean(right * right, axis=-1, keepdims=True) + EPSILON
        norms = size * pltpu.roll(size, 2, 0)
        score = inner / jnp.sqrt(norms) / SOFTMAX_WARMTH
        number = row + lax.broadcasted_iota(jnp.int32, (256, 128), 0)
        for k in range(8):
            hit = target[pl.ds(k, 1)] == number
            out[k] += jnp.sum(jnp.where(hit, score, 0.0), axis=0, keepdims=True)
        return carry

    lax.fori_loop(0, (steps + 31) // 32, finish, 0)


def score_pairs(sa, sb, sa_mix, sb_mix, plist, w_pool):
    samples, features = sa.shape[1:]
    vmem = pl.BlockSpec(memory_space=pltpu.VMEM)
    two = 2 * samples
    return pl.pallas_call(
        score_kernel,
        out_shape=pltpu.VMEM((8, 1, 128), jnp.float32),
        in_specs=[vmem] * 5 + [pl.BlockSpec(memory_space=pltpu.HBM)],
        out_specs=vmem,
        scratch_shapes=[
            pltpu.VMEM(w_pool.shape, jnp.bfloat16),
            pltpu.VMEM((GROUP // 2, two, two), jnp.float32),
            pltpu.VMEM((GROUP // 2, 2 * two, 2 * two), jnp.bfloat16),
            pltpu.VMEM((2 * CAPACITY, features), jnp.float32),
            pltpu.VMEM((8, 128), jnp.int32),
            pltpu.VMEM((3, 1, CAPACITY), jnp.int32),
            pltpu.SMEM((3, 1, CAPACITY), jnp.int32),
            pltpu.SemaphoreType.DMA,
            pltpu.SemaphoreType.DMA,
        ],
        compiler_params=pltpu.CompilerParams(vmem_limit_bytes=16 << 20),
        name="score_pairs",
    )(sa, sb, sa_mix, sb_mix, plist, w_pool)


def return_kernel(part, out, landed, send_sem, recv_sem):
    x, y, z, core = place()
    me = z * 8 + y * 2 + core

    def partner(k):
        return lax.rem(x + k // 4, 4), lax.rem(y + k % 4, 4)

    barrier = pltpu.get_barrier_semaphore()
    for k in range(1, 16):
        tx, ty = partner(k)
        pl.semaphore_signal(
            barrier, inc=1, device_id=(tx, z * 8 + ty * 2 + core), device_id_type=MESH
        )
    pl.semaphore_wait(barrier, 15)
    sent = []
    for k in range(1, 16):
        tx, ty = partner(k)
        copy = pltpu.make_async_remote_copy(
            src_ref=part.at[tx * 2 + ty // 2], dst_ref=landed.at[k],
            send_sem=send_sem.at[k], recv_sem=recv_sem.at[k],
            device_id=(tx, z * 8 + ty * 2 + core), device_id_type=MESH,
        )
        copy.start()
        sent.append(copy)
    total = part[x * 2 + y // 2]
    for k, copy in enumerate(sent, start=1):
        copy.wait_recv()
        total = total + landed[k]
    half = jnp.where(lax.rem(y, 2) == 0, total, pltpu.roll(total, 64, 1))
    out[...] = half[:, :64]
    for copy in sent:
        copy.wait_send()


def return_scores(part):
    vmem = pl.BlockSpec(memory_space=pltpu.VMEM)
    return pl.pallas_call(
        return_kernel,
        out_shape=jax.ShapeDtypeStruct((1, 64), jnp.float32),
        in_specs=[vmem],
        out_specs=vmem,
        scratch_shapes=[
            pltpu.VMEM((16, 1, 128), jnp.float32),
            pltpu.SemaphoreType.DMA((16,)),
            pltpu.SemaphoreType.DMA((16,)),
        ],
        compiler_params=pltpu.CompilerParams(
            collective_id=1, has_side_effects=True, vmem_limit_bytes=1 << 20
        ),
        name="return_scores",
    )(part)


def local(cells, w_cell, w_mix, w_pool, pairs, counts):
    in_place = lambda v: pltpu.with_memory_space_constraint(v, pltpu.HBM)
    cells, w_cell, w_mix, w_pool = map(in_place, (cells, w_cell, w_mix, w_pool))
    blocks = gather_blocks(cells, w_cell, w_mix, in_place(pairs.T), counts)
    return return_scores(score_pairs(*blocks, w_pool)).reshape(pairs.shape[0])


def solution(mesh):
    placed = (P("shard", None, None), P(), P(), P(), P(("grp", "shard"), None), P(("grp", "shard")))
    return jax.shard_map(
        local, mesh=mesh, in_specs=placed, out_specs=P(("grp", "shard")), check_vma=False
    )
```

```python
import functools
import math

import jax
import jax.numpy as jnp
from jax import lax
from jax.experimental import pallas as pl
from jax.experimental.pallas import tpu as pltpu
from jax.sharding import PartitionSpec as P

SOFTMAX_WARMTH = 0.07
EPSILON = 1e-06
MESH = pl.DeviceIdType.MESH
CAPACITY = 512
GROUP = 4


def place():
    x = lax.axis_index("grp")
    shard = lax.axis_index("shard")
    return x, lax.rem(shard // 2, 4), shard // 8, lax.rem(shard, 2)


def gather_kernel(
    cells, w_cell, w_mix, pairs, live, sa, sb, sa_mix, sb_mix, plist, stage, cell_w, mix_w,
    ids, send_sem, recv_sem, local_sem
):
    columns, samples, features = stage.shape
    x, y, z, core = place()
    quarter_at = lambda k: pl.ds(4 * lax.rem(x + k, 4), 4)
    thirds = range(0, features, 256)
    moves = [(pairs, ids), (cells.at[quarter_at(0)], stage.at[quarter_at(0)])]
    moves += [(w_cell.at[:, pl.ds(f, 256)], cell_w.at[:, pl.ds(f, 256)]) for f in thirds]
    moves += [(cells.at[quarter_at(k)], stage.at[quarter_at(k)]) for k in (1, 2, 3)]
    moves += [(w_mix, mix_w)]
    loads = [
        pltpu.make_async_copy(src, dst, local_sem.at[k]) for k, (src, dst) in enumerate(moves)
    ]
    for copy in loads:
        copy.start()

    shard = lambda z_, y_, c_: z_ * 8 + y_ * 2 + c_
    xr, xl = lax.rem(x + 1, 4), lax.rem(x + 3, 4)
    yr, yl, yo = lax.rem(y + 1, 4), lax.rem(y + 3, 4), lax.rem(y + 2, 4)
    zs = [lax.rem(z + k, 8) for k in range(8)]
    me = shard(z, y, core)
    dev = {
        "x+": (xr, me),
        "x-": (xl, me),
        "y+": (x, shard(z, yr, core)),
        "y-": (x, shard(z, yl, core)),
        "z+": (x, shard(zs[1], y, core)),
        "z-": (x, shard(zs[7], y, core)),
        "c": (x, shard(z, y, 1 - core)),
    }
    barrier = pltpu.get_barrier_semaphore()
    for d in dev.values():
        pl.semaphore_signal(barrier, inc=1, device_id=d, device_id_type=MESH)

    def project(k):
        quarter = lax.rem(x + k, 4)
        loads[1 if k == 0 else 4 + k].wait()
        rows = stage[pl.ds(quarter * 4, 4)].reshape(4 * samples, features)
        for third, first in enumerate(thirds):
            if k == 0:
                loads[2 + third].wait()
            block = jnp.dot(
                rows, cell_w[:, pl.ds(first, 256)], preferred_element_type=jnp.float32
            ).astype(jnp.bfloat16)
            sa[pl.ds(y * 16 + quarter * 4, 4), :, pl.ds(first, 256)] = block.reshape(4, samples, 256)

    project(0)
    sb[pl.ds(z * 8 + core * 4, 4)] = sa[pl.ds(y * 16 + 4 * x, 4)]
    loads[0].wait()
    first_id, second_id = ids[pl.ds(0, 1)], ids[pl.ds(1, 1)]
    slot = lax.broadcasted_iota(jnp.int32, first_id.shape, 1)
    row = jnp.where(slot < live[0], y * 16 + (first_id & 15) + 64 * second_id, -1)
    row = jnp.concatenate([row, jnp.full(row.shape, -1, jnp.int32)], axis=1)
    plist[x, y] = jnp.where(lax.rem(y, 2) == 0, row, pltpu.roll(row, 64, 1))

    pl.semaphore_wait(barrier, len(dev))

    kinds = {}
    sent = []

    def index_of(kind):
        return kinds.setdefault(kind, len(kinds))

    def send(kind, src, dst, to):
        k = index_of(kind)
        copy = pltpu.make_async_remote_copy(
            src_ref=src, dst_ref=dst, send_sem=send_sem.at[k], recv_sem=recv_sem.at[k],
            device_id=dev[to], device_id_type=MESH,
        )
        copy.start()
        sent.append(copy)

    def arrive(kind, slot, to):
        k = index_of(kind)
        pltpu.make_async_remote_copy(
            src_ref=slot, dst_ref=slot, send_sem=send_sem.at[k], recv_sem=recv_sem.at[k],
            device_id=dev[to], device_id_type=MESH,
        ).wait_recv()

    def a_cols(y_, first, size):
        return sa.at[pl.ds(y_ * 16 + first, size)]

    def b_cols(z_, c_, first, size):
        return sb.at[pl.ds(z_ * 8 + c_ * 4 + first, size)]

    def times_mix(*runs):
        rows = jnp.concatenate([source[pl.ds(at, size)] for source, _, at, size in runs], axis=0)
        rows = rows.reshape(-1, features)
        for first in thirds:
            block = jnp.dot(
                rows, mix_w[:, pl.ds(first, 256)], preferred_element_type=jnp.float32
            ).astype(jnp.bfloat16).reshape(-1, samples, 256)
            done = 0
            for _, result, at, size in runs:
                result[pl.ds(at, size), :, pl.ds(first, 256)] = block[done : done + size]
                done += size

    def some_a(y_, half):
        return [(sa, sa_mix, y_ * 16 + 2 * half + 4 * q, 2) for q in range(4)]

    def some_b(z_, c_):
        return [(sb, sb_mix, z_ * 8 + c_ * 4, 4)]

    def own_b(d):
        return some_b(zs[8 - d], core) + some_b(zs[d], core)

    def products(z_, c_):
        return sb_mix.at[pl.ds(z_ * 8 + c_ * 4, 4)]

    def send_products(d):
        for sign, z_ in (("+", zs[8 - d]), ("-", zs[d])):
            send(f"m{sign}{d}", products(z_, core), products(z_, core), "c")

    def direct(y_, k):
        return a_cols(y_, 4 * lax.rem(x + k, 4) + 2, 2)

    def last(y_, k):
        return a_cols(y_, 4 * lax.rem(x + k, 4) + 3, 1)

    shared = a_cols(y, 4 * x, 2)
    for p in (0, 1):
        send(f"z+0{p}", b_cols(z, core, 2 * p, 2), b_cols(z, core, 2 * p, 2), "z+")
        send(f"z-0{p}", b_cols(z, core, 2 * (1 - p), 2), b_cols(z, core, 2 * (1 - p), 2), "z-")
        if p == 0:
            send("y+S", shared, shared, "y+")
            send("y-S", shared, shared, "y-")
    send("l+", plist.at[x, y], plist.at[x, y], "y+")
    send("l-", plist.at[x, y], plist.at[x, y], "y-")
    send("y+D0", direct(y, 0), direct(y, 0), "y+")
    send("y-D0", direct(y, 0), direct(y, 0), "y-")
    send("c0", b_cols(z, core, 0, 4), b_cols(z, core, 0, 4), "c")
    project(1)
    send("y-D1", direct(y, 1), direct(y, 1), "y-")
    project(2)
    project(3)
    loads[8].wait()
    other = 1 - core
    arrive_c0 = lambda: arrive("c0", b_cols(z, other, 0, 4), "c")

    def arrive_c(d, p):
        arrive(f"c+{d}{p}", b_cols(zs[8 - d], other, 2 * p, 2), "c")
        arrive(f"c-{d}{p}", b_cols(zs[d], other, 2 * (1 - p), 2), "c")

    def z_round(d, p):
        up = b_cols(zs[8 - d], core, 2 * p, 2)
        down = b_cols(zs[d], core, 2 * (1 - p), 2)
        arrive(f"z+{d - 1}{p}", up, "z-")
        if d < 3 or (d == 3 and p == 0):
            send(f"z+{d}{p}", up, up, "z+")
        send(f"c+{d}{p}", up, up, "c")
        arrive(f"z-{d - 1}{p}", down, "z+")
        if d < 3 or (d == 3 and p == 0):
            send(f"z-{d}{p}", down, down, "z-")
        send(f"c-{d}{p}", down, down, "c")

    times_mix(*some_b(z, core), *some_a(y, 0))
    times_mix(*some_a(y, 1))
    send("m0", products(z, core), products(z, core), "c")

    below, above = a_cols(yl, 4 * x, 2), a_cols(yr, 4 * x, 2)
    arrive("y+S", below, "y-")
    send("y+S2", below, below, "y+")
    send("x+b", below, below, "x+")
    send("x-b", below, below, "x-")
    arrive("y-S", above, "y+")
    send("x+a", above, above, "x+")
    send("x-a", above, above, "x-")
    arrive("l+", plist.at[x, yl], "y-")
    send("l+2", plist.at[x, yl], plist.at[x, yl], "y+")
    arrive("l-", plist.at[x, yr], "y+")
    z_round(1, 0)

    arrive("y+D0", direct(yl, 0), "y-")
    send("y+c", a_cols(yl, 4 * x + 2, 1), a_cols(yl, 4 * x + 2, 1), "y+")
    for k in (1, 2, 3):
        send(f"y+D{k}", direct(y, k), direct(y, k), "y+")
    arrive("y-D0", direct(yr, 0), "y+")
    send("y-r0", last(yr, 0), last(yr, 0), "y-")
    send("y-D2", direct(y, 2), direct(y, 2), "y-")
    z_round(1, 1)
    arrive("l+2", plist.at[x, yo], "y-")
    send("lx+", plist.at[x], plist.at[x], "x+")
    send("lx-", plist.at[x], plist.at[x], "x-")
    times_mix(*own_b(1))

    arrive("y+S2", a_cols(yo, 4 * x, 2), "y-")
    for j in (0, 1):
        one, two = a_cols(yo, 4 * x + j, 1), a_cols(yo, 4 * x + 1 - j, 1)
        send(f"x+f{j}", one, one, "x+")
        send(f"x-f{1 - j}", two, two, "x-")
    z_round(2, 0)
    got = a_cols(yl, 4 * xl, 2)
    arrive("x+b", got, "x-")
    send("x+b2", got, got, "x+")
    arrive("y-D1", direct(yr, 1), "y+")
    send("y-r1", last(yr, 1), last(yr, 1), "y-")
    send("y-D3", direct(y, 3), direct(y, 3), "y-")
    got = a_cols(yr, 4 * xr, 2)
    arrive("x-a", got, "x+")
    send("x-a2", got, got, "x-")
    arrive("lx+", plist.at[xl], "x-")
    send("lx+2", plist.at[xl], plist.at[xl], "x+")
    arrive("y+c", a_cols(yo, 4 * x + 2, 1), "y-")
    for to in ("x+", "x-"):
        send(to + "c", a_cols(yo, 4 * x + 2, 1), a_cols(yo, 4 * x + 2, 1), to)
    z_round(2, 1)

    times_mix(*own_b(2))
    send_products(1)
    early = len(sent)
    arrive("y-D2", direct(yr, 2), "y+")
    send("y-r2", last(yr, 2), last(yr, 2), "y-")
    got = a_cols(yo, 4 * xl, 1)
    arrive("x+f0", got, "x-")
    send("x+f02", got, got, "x+")
    got = a_cols(yo, 4 * xr + 1, 1)
    arrive("x-f1", got, "x+")
    send("x-f12", got, got, "x-")
    z_round(3, 0)
    xo = lax.rem(x + 2, 4)
    arrive("x-b", a_cols(yl, 4 * xr, 2), "x+")
    arrive("x+a", a_cols(yr, 4 * xl, 2), "x-")
    arrive("x+b2", a_cols(yl, 4 * xo, 2), "x-")
    arrive("x-a2", a_cols(yr, 4 * xo, 2), "x+")
    for far_y in (yl, yr):
        times_mix(*some_a(far_y, 0))
    send_products(2)
    got = a_cols(yo, 4 * xl + 2, 1)
    arrive("x+c", got, "x-")
    send("x+c2", got, got, "x+")
    z_round(3, 1)
    arrive("y-D3", direct(yr, 3), "y+")
    send("y-r3", last(yr, 3), last(yr, 3), "y-")
    times_mix(*some_a(yr, 1), *own_b(3))
    send_products(3)
    for copy in sent[:early]:
        copy.wait_send()
    late = sent[early:]

    z_round(4, 0)
    arrive("x-c", a_cols(yo, 4 * xr + 2, 1), "x+")
    arrive("x+c2", a_cols(yo, 4 * xo + 2, 1), "x-")
    for k in range(4):
        arrive(f"y-r{k}", last(yo, k), "y+")
    for k in (1, 2, 3):
        arrive(f"y+D{k}", direct(yl, k), "y-")
    arrive("x+f1", a_cols(yo, 4 * xl + 1, 1), "x-")
    arrive("x-f0", a_cols(yo, 4 * xr, 1), "x+")
    arrive("x+f02", a_cols(yo, 4 * xo, 1), "x-")
    arrive("x-f12", a_cols(yo, 4 * xo + 1, 1), "x+")
    times_mix(*some_a(yl, 1), *some_a(yo, 0), *some_a(yo, 1), *some_b(zs[4], core))
    for copy in late:
        copy.wait_send()
    arrive("lx-", plist.at[xr], "x+")
    arrive("lx+2", plist.at[xo], "x-")
    arrive_c0()
    arrive("m0", products(z, other), "c")
    for d in (1, 2, 3):
        arrive_c(d, 0)
        arrive_c(d, 1)
        arrive(f"m+{d}", products(zs[8 - d], other), "c")
        arrive(f"m-{d}", products(zs[d], other), "c")
    arrive_c(4, 0)
    times_mix(*some_b(zs[4], other))
    del sent[:-2]
    for copy in sent:
        copy.wait_send()
    assert len(kinds) <= COPIES


COPIES = 96


def gather_blocks(cells, w_cell, w_mix, pairs, counts):
    vmem = pl.BlockSpec(memory_space=pltpu.VMEM)
    columns, samples, features = cells.shape
    blocks = pltpu.VMEM((64, samples, features), jnp.bfloat16)
    return pl.pallas_call(
        gather_kernel,
        out_shape=(blocks,) * 4 + (pltpu.VMEM((4, 4, 1, 128), jnp.int32),),
        in_specs=[pl.BlockSpec(memory_space=pltpu.HBM)] * 4 + [pl.BlockSpec(memory_space=pltpu.SMEM)],
        out_specs=(vmem,) * 5,
        scratch_shapes=[
            pltpu.VMEM((columns, samples, features), jnp.bfloat16),
            pltpu.VMEM(w_cell.shape, jnp.bfloat16),
            pltpu.VMEM(w_mix.shape, jnp.bfloat16),
            pltpu.VMEM(pairs.shape, jnp.int32),
            pltpu.SemaphoreType.DMA((COPIES,)),
            pltpu.SemaphoreType.DMA((COPIES,)),
            pltpu.SemaphoreType.DMA((9,)),
        ],
        compiler_params=pltpu.CompilerParams(
            collective_id=0, has_side_effects=True, vmem_limit_bytes=12 << 20
        ),
        name="gather_blocks",
    )(cells, w_cell, w_mix, pairs, counts)


def add_scores(vectors, row, pool_w, target, out):
    right = jnp.dot(vectors, pool_w[...], preferred_element_type=jnp.float32)
    left = pltpu.roll(right, 2, 0)
    inner = jnp.mean(left * right, axis=-1, keepdims=True)
    size = jnp.mean(right * right, axis=-1, keepdims=True) + EPSILON
    norms = size * pltpu.roll(size, 2, 0)
    score = inner / jnp.sqrt(norms) / SOFTMAX_WARMTH
    number = row + lax.broadcasted_iota(jnp.int32, (256, 128), 0)
    for k in range(8):
        hit = target[pl.ds(k, 1)] == number
        out[k] += jnp.sum(jnp.where(hit, score, 0.0), axis=0, keepdims=True)


def score_kernel(
    sa, sb, sa_mix, sb_mix, plist, w_pool, out, head, target, pool_w,
    raw, blend, pooled, table, lst, sem, list_sem
):
    samples, features = sa.shape[1:]
    scale = 1.0 / math.sqrt(features)
    load = pltpu.make_async_copy(w_pool, pool_w, sem)
    load.start()

    x, y, _, _ = place()
    codes = jnp.concatenate(
        [jnp.maximum(plist[k // 2, k % 2 * 2], plist[k // 2, k % 2 * 2 + 1]) for k in range(8)],
        axis=0,
    )
    b_id = codes >> 6
    mine = (codes >= 0) & (((b_id >> 5) & 3) == y) & (((b_id >> 2) & 3) == x)
    flag = jnp.where(mine, 1.0, 0.0)
    row_id = lax.broadcasted_iota(jnp.int32, (8, 128), 0)
    lane = lambda n: lax.broadcasted_iota(jnp.int32, (128, n), 1)
    upto = jnp.where(lax.broadcasted_iota(jnp.int32, (128, 128), 0) < lane(128), 1.0, 0.0)
    ahead = jnp.dot(
        flag.astype(jnp.bfloat16), upto.astype(jnp.bfloat16), preferred_element_type=jnp.float32
    )
    rows_upto = jnp.broadcast_to(jnp.sum(flag, axis=1, keepdims=True), (8, 128))
    own = rows_upto
    for shift in (1, 2, 4):
        rows_upto = rows_upto + jnp.where(
            row_id >= shift, pltpu.roll(rows_upto, shift, 0), 0.0
        )
    position = jnp.where(mine, (ahead + rows_upto - own).astype(jnp.int32), -1)
    target[...] = jnp.where(
        mine, 8 * (position >> 2) + 4 * ((position >> 1) & 1) + 2 + (position & 1), -1
    )
    spread = position.T
    a_at = (codes & 63).astype(jnp.bfloat16)
    b_at = ((b_id >> 7) * 8 + ((b_id >> 4) & 1) * 4 + (b_id & 3)).astype(jnp.bfloat16)
    found_a = jnp.zeros((8, CAPACITY), jnp.float32)
    found_b = jnp.zeros((8, CAPACITY), jnp.float32)
    for k in range(8):
        hit = jnp.where(spread[:, k : k + 1] == lane(CAPACITY), 1.0, 0.0).astype(jnp.bfloat16)
        keep = row_id == k
        both = jnp.concatenate(
            [jnp.where(keep, a_at, 0), jnp.where(keep, b_at, 0)], axis=0
        ).astype(jnp.bfloat16)
        got = jnp.dot(both, hit, preferred_element_type=jnp.float32)
        found_a = found_a + got[:8]
        found_b = found_b + got[8:]
    sum_rows = lambda v: jnp.sum(v, axis=0, keepdims=True).astype(jnp.int32)
    total = jnp.broadcast_to(rows_upto[7:, :1], (1, CAPACITY)).astype(jnp.int32)
    table[0] = sum_rows(found_a)
    table[1] = sum_rows(found_b)
    table[2] = total
    move = pltpu.make_async_copy(table, lst, list_sem)
    move.start()
    move.wait()
    count = lst[2, 0, 0]
    steps = (count + GROUP - 1) // GROUP

    two = 2 * samples
    same = (
        lax.broadcasted_iota(jnp.int32, (two, two), 0) // samples
        == lax.broadcasted_iota(jnp.int32, (two, two), 1) // samples
    )
    identity = jnp.where(
        lax.broadcasted_iota(jnp.int32, (two, two), 0) == lax.broadcasted_iota(jnp.int32, (two, two), 1),
        1.0, 0.0,
    ).astype(jnp.bfloat16)
    for h in range(GROUP // 2):
        blend[h, pl.ds(0, two), pl.ds(0, two)] = identity
        blend[h, pl.ds(two, two), pl.ds(two, two)] = identity

    def pair_rows(source, which, step, h):
        first = step * GROUP + 2 * h
        return jnp.concatenate(
            [source[lst[which, 0, first]], source[lst[which, 0, first + 1]]], axis=0
        )

    def scores(step, h):
        found = lax.dot_general(
            pair_rows(sa, 0, step, h), pair_rows(sb, 1, step, h), (((1,), (1,)), ((), ())),
            preferred_element_type=jnp.float32,
        )
        return jnp.where(same, found * scale, -1e30)

    def attend(found, axis):
        weight = jnp.exp(found - jnp.max(found, axis=axis, keepdims=True))
        return weight * (1.0 / jnp.sum(weight, axis=axis, keepdims=True))

    def keep_weights(found, h):
        blend[h, pl.ds(0, two), pl.ds(two, two)] = attend(found, 1).astype(jnp.bfloat16)
        blend[h, pl.ds(two, two), pl.ds(0, two)] = attend(found, 0).T.astype(jnp.bfloat16)

    def pool(step):
        products = [
            jnp.concatenate(
                [pair_rows(sa_mix, 0, step, h), pair_rows(sb_mix, 1, step, h)], axis=0
            )
            for h in range(GROUP // 2)
        ]
        row = pl.multiple_of(step * 2 * GROUP, 2 * GROUP)
        for first in range(0, features, 256):
            means = []
            for h in range(GROUP // 2):
                hidden = jnp.tanh(
                    jnp.dot(
                        blend[h], products[h][:, first : first + 256],
                        preferred_element_type=jnp.float32,
                    )
                )
                means.append(jnp.sum(hidden.reshape(4, samples, 256), axis=1) * (1.0 / samples))
            pooled[pl.ds(row, 2 * GROUP), pl.ds(first, 256)] = jnp.concatenate(means, axis=0)

    halves = range(GROUP // 2)

    def keep_scores(step):
        for h in halves:
            raw[h] = scores(step, h)

    def one_step(step):
        now = [raw[h] for h in halves]
        pool(step - 1)
        for h in halves:
            keep_weights(now[h], h)
        keep_scores(jnp.minimum(step + 1, steps - 1))

    def two_steps(turn, carry):
        one_step(2 * turn + 1)
        one_step(2 * turn + 2)
        return carry

    @pl.when(steps > 0)
    def _():
        keep_scores(0)
        for h in halves:
            keep_weights(raw[h], h)
        keep_scores(jnp.minimum(1, steps - 1))
        lax.fori_loop(0, (steps - 1) // 2, two_steps, 0)
        pl.when(lax.rem(steps, 2) == 0)(lambda: one_step(steps - 1))
        pool(steps - 1)

    load.wait()
    out[...] = jnp.zeros_like(out)
    head[...] = pooled[pl.ds(0, 256)].astype(jnp.bfloat16)

    def finish(chunk, carry):
        row = pl.multiple_of(chunk * 256, 256)
        add_scores(pooled[pl.ds(row, 256)].astype(jnp.bfloat16), row, pool_w, target, out)
        return carry

    lax.fori_loop(1, (steps + 31) // 32, finish, 0)


def score_pairs(sa, sb, sa_mix, sb_mix, plist, w_pool):
    samples, features = sa.shape[1:]
    vmem = pl.BlockSpec(memory_space=pltpu.VMEM)
    two = 2 * samples
    return pl.pallas_call(
        score_kernel,
        out_shape=(
            pltpu.VMEM((8, 1, 128), jnp.float32),
            pltpu.VMEM((256, features), jnp.bfloat16),
            pltpu.VMEM((8, 128), jnp.int32),
            pltpu.VMEM(w_pool.shape, jnp.bfloat16),
        ),
        in_specs=[vmem] * 5 + [pl.BlockSpec(memory_space=pltpu.HBM)],
        out_specs=(vmem,) * 4,
        scratch_shapes=[
            pltpu.VMEM((GROUP // 2, two, two), jnp.float32),
            pltpu.VMEM((GROUP // 2, 2 * two, 2 * two), jnp.bfloat16),
            pltpu.VMEM((2 * CAPACITY, features), jnp.float32),
            pltpu.VMEM((3, 1, CAPACITY), jnp.int32),
            pltpu.SMEM((3, 1, CAPACITY), jnp.int32),
            pltpu.SemaphoreType.DMA,
            pltpu.SemaphoreType.DMA,
        ],
        compiler_params=pltpu.CompilerParams(vmem_limit_bytes=16 << 20),
        name="score_pairs",
    )(sa, sb, sa_mix, sb_mix, plist, w_pool)


def return_kernel(rest, head, target, pool_w, out, part, landed, send_sem, recv_sem):
    x, y, z, core = place()
    me = z * 8 + y * 2 + core

    def partner(k):
        return lax.rem(x + k // 4, 4), lax.rem(y + k % 4, 4)

    barrier = pltpu.get_barrier_semaphore()
    for k in range(1, 16):
        tx, ty = partner(k)
        pl.semaphore_signal(
            barrier, inc=1, device_id=(tx, z * 8 + ty * 2 + core), device_id_type=MESH
        )
    part[...] = rest[...]
    add_scores(head[...], 0, pool_w, target, part)
    pl.semaphore_wait(barrier, 15)
    sent = []
    for k in range(1, 16):
        tx, ty = partner(k)
        copy = pltpu.make_async_remote_copy(
            src_ref=part.at[tx * 2 + ty // 2], dst_ref=landed.at[k],
            send_sem=send_sem.at[k], recv_sem=recv_sem.at[k],
            device_id=(tx, z * 8 + ty * 2 + core), device_id_type=MESH,
        )
        copy.start()
        sent.append(copy)
    total = part[x * 2 + y // 2]
    for k, copy in enumerate(sent, start=1):
        copy.wait_recv()
        total = total + landed[k]
    half = jnp.where(lax.rem(y, 2) == 0, total, pltpu.roll(total, 64, 1))
    out[...] = half[:, :64]
    for copy in sent:
        copy.wait_send()


def return_scores(*parts):
    vmem = pl.BlockSpec(memory_space=pltpu.VMEM)
    return pl.pallas_call(
        return_kernel,
        out_shape=jax.ShapeDtypeStruct((1, 64), jnp.float32),
        in_specs=[vmem] * 4,
        out_specs=vmem,
        scratch_shapes=[
            pltpu.VMEM((8, 1, 128), jnp.float32),
            pltpu.VMEM((16, 1, 128), jnp.float32),
            pltpu.SemaphoreType.DMA((16,)),
            pltpu.SemaphoreType.DMA((16,)),
        ],
        compiler_params=pltpu.CompilerParams(
            collective_id=1, has_side_effects=True, vmem_limit_bytes=8 << 20
        ),
        name="return_scores",
    )(*parts)


def local(cells, w_cell, w_mix, w_pool, pairs, counts):
    in_place = lambda v: pltpu.with_memory_space_constraint(v, pltpu.HBM)
    cells, w_cell, w_mix, w_pool = map(in_place, (cells, w_cell, w_mix, w_pool))
    blocks = gather_blocks(cells, w_cell, w_mix, in_place(pairs.T), counts)
    return return_scores(*score_pairs(*blocks, w_pool)).reshape(pairs.shape[0])


def solution(mesh):
    placed = (P("shard", None, None), P(), P(), P(), P(("grp", "shard"), None), P(("grp", "shard")))
    return jax.shard_map(
        local, mesh=mesh, in_specs=placed, out_specs=P(("grp", "shard")), check_vma=False
    )
```
